128 devices in a mesh: store: 32 (over z, x, core), tensor: 4 (over y).
Axes of the slice: x: 4, y: 4, z: 4, core: 2. Of those that a mesh axis runs over, the one named last changes fastest.
Arguments:
- eval_inputs: bfloat16 [24576, 4096], P('store'), may hold values from -6 to 6
- eval_grads: bfloat16 [24576, 4096], P('store'), may hold values from -6 to 6
- w_gate: bfloat16 [4096, 7168], P('store', 'tensor'), may hold values from -0.09375 to 0.09375
- w_down: bfloat16 [7168, 4096], P('tensor', 'store'), may hold values from -0.0625 to 0.0625
- proj_in: bfloat16 [4096, 64], replicated, may hold values from -0.09375 to 0.09375
- proj_out: bfloat16 [7168, 64], P('tensor'), may hold values from -0.0625 to 0.0625
- store_rows: bfloat16 [131072, 4096], P('store', 'tensor'), may hold values from -3 to 3
- eval_strata: int32 [192], replicated, may hold values from 0 to 7, as said below
- block_strata: int32 [1024], P('store'), may hold values from 0 to 7
Outputs:
- scores: float32 [192, 131072], P('tensor', 'store')
The draws below stay inside these ranges and needn't reach their ends.
Inputs may be any that keep to these rules, and one draw needn't show every extreme that they name: `eval_strata`: each of the 8 strata is named by exactly 24 evaluation sequences.
All inputs are finite; a program needn't handle non-finite values.
Results may differ from the reference program's by a relative error of at most 0.0041.
Values may be sent and summed in bfloat16 or wider, within the bound.
A program may use at most 192 MiB of HBM per device.

```python
import math
import jax
import jax.numpy as jnp
import numpy as np
from jax import lax

D = 4096
FF_WIN = 7168
RANK = 64
SEQ_LEN = 128
BLOCK = 128
STRATA = 8
EVAL = 192
TOKENS = 24576
ROWS = 131072
NBLOCKS = 1024
FEATURES = 4096


def draw_eval_strata(key, part):
    shuffled = jax.random.permutation(jax.random.fold_in(key, 17), EVAL)
    return (shuffled % STRATA).astype(jnp.int32)


def touch_ends(values, key, least, high):
    spot = [jax.random.randint(jax.random.fold_in(key, axis), (), 0, length) for axis, length in enumerate(values.shape)]
    main_axis = values.shape.index(max(values.shape))
    beside = spot[:main_axis] + [(spot[main_axis] + 1) % values.shape[main_axis]] + spot[main_axis + 1:]
    return values.at[tuple(spot)].set(least).at[tuple(beside)].set(high)


def steps_of(stream_key, extent, split, low, largest):
    factor_of = 1.0
    for position, shards_of in split:
        steps = jax.random.uniform(jax.random.fold_in(jax.random.fold_in(stream_key, 6), position), (shards_of,), jnp.float32, low / len(split), largest / len(split))
        factor_of = factor_of * jnp.repeat(jnp.exp(steps), extent[position] // shards_of).reshape((-1,) + (1,) * (len(extent) - 1 - position))
    return factor_of


def rank_table(number_of, skew):
    weights = [(1 << 20) // math.isqrt(standing ** skew) + 1 for standing in range(1, number_of + 1)]
    spread = 1 + sum(weights) // (1 << 30)
    return np.cumsum(np.array([max(1, weight // spread) for weight in weights]))


def ranked_ids(rng, shape, number_of, skew):
    listing = rank_table(number_of, skew)
    lot = jax.random.randint(jax.random.fold_in(rng, 1), shape, 0, int(listing[number_of - 1]))
    rank = jnp.searchsorted(jnp.asarray(listing, jnp.int32), lot, side="right")
    return jax.random.permutation(jax.random.fold_in(rng, 2), number_of)[rank].astype(jnp.int32)


def bell_draw(stream_key, dims, deviation, most, pieces=(), kind=jnp.bfloat16):
    drawn = jax.random.normal(stream_key, dims, jnp.float32) * deviation
    if len(pieces) > 0:
        drawn = steps_of(stream_key, dims, pieces, -0.22, 0.18) * drawn
    return jnp.clip(drawn, min=-most, max=most).astype(kind)


def setup_inputs(seed: int = 0) -> dict:
    key_of = jax.random.split(jax.random.key(seed), 10)
    return {
        "eval_inputs": bell_draw(key_of[0], (TOKENS, D), 1.0, 6.0, ((0, 32),)),
        "eval_grads": bell_draw(key_of[1], (TOKENS, D), 1.0, 6.0, ((0, 32),)),
        "w_gate": bell_draw(key_of[2], (D, FF_WIN), D ** -0.5, 0.09375, ((0, 32), (1, 4))),
        "w_down": bell_draw(key_of[3], (FF_WIN, D), FF_WIN ** -0.5, 0.0625, ((0, 4), (1, 32))),
        "proj_in": bell_draw(key_of[4], (D, RANK), D ** -0.5, 0.09375),
        "proj_out": bell_draw(key_of[5], (FF_WIN, RANK), FF_WIN ** -0.5, 0.0625, ((0, 4),)),
        "store_rows": bell_draw(key_of[6], (ROWS, FEATURES), 0.5, 3.0, ((0, 32), (1, 4))),
        "eval_strata": draw_eval_strata(jax.random.fold_in(key_of[9], 71), 0),
        "block_strata": touch_ends(ranked_ids(key_of[8], (NBLOCKS,), STRATA, 2), jax.random.fold_in(key_of[8], 3), 0, STRATA - 1).astype(jnp.int32),
    }


def group_grads(inputs_grp, grads_grp, w_gate32, w_down32, proj_in32, proj_out32):
    inputs32 = inputs_grp.astype(jnp.float32)
    grads32 = grads_grp.astype(jnp.float32)
    gate_pre = jnp.dot(inputs32, w_gate32, precision=lax.Precision.HIGHEST)
    back_pre = jnp.dot(grads32, w_down32.T, precision=lax.Precision.HIGHEST)
    update_bf = (back_pre * jax.nn.silu(gate_pre)).astype(jnp.bfloat16)
    left_proj = jnp.dot(inputs32, proj_in32, precision=lax.Precision.HIGHEST)
    right_proj = jnp.dot(update_bf.astype(jnp.float32), proj_out32, precision=lax.Precision.HIGHEST)
    left_seq = left_proj.reshape(STRATA, SEQ_LEN, RANK)
    right_seq = right_proj.reshape(STRATA, SEQ_LEN, RANK)
    outer_sum = jnp.einsum("sti,stj->sij", left_seq, right_seq, precision=lax.Precision.HIGHEST) / SEQ_LEN
    return outer_sum.reshape(STRATA, RANK * RANK)


def reference(eval_inputs, eval_grads, w_gate, w_down, proj_in, proj_out, store_rows, eval_strata, block_strata):
    groups = EVAL // STRATA
    inputs_grp = eval_inputs.reshape(groups, STRATA * SEQ_LEN, D)
    grads_grp = eval_grads.reshape(groups, STRATA * SEQ_LEN, D)
    w_gate32 = w_gate.astype(jnp.float32)
    w_down32 = w_down.astype(jnp.float32)
    proj_in32 = proj_in.astype(jnp.float32)
    proj_out32 = proj_out.astype(jnp.float32)

    def per_group(paired):
        return group_grads(paired[0], paired[1], w_gate32, w_down32, proj_in32, proj_out32)

    flat_grads = lax.map(per_group, (inputs_grp, grads_grp)).reshape(EVAL, RANK * RANK).astype(jnp.bfloat16)
    raw_scores = jnp.dot(flat_grads.astype(jnp.float32), store_rows.astype(jnp.float32).T, precision=lax.Precision.HIGHEST)
    row_strata = jnp.repeat(block_strata, BLOCK)
    matched = eval_strata[:, None] == row_strata[None, :]
    return jnp.where(matched, raw_scores, jnp.zeros_like(raw_scores))
```

```python
import functools

import jax
import jax.numpy as jnp
from jax import lax
from jax.experimental import pallas as pl
from jax.experimental.pallas import tpu as pltpu
from jax.sharding import PartitionSpec as P

MESH = pl.DeviceIdType.MESH
RANK, SEQ, BLOCK, STRATA = 64, 128, 128, 8
PER = 24
PAD = 32
CHUNK = 256
AHEAD1, AHEAD2, AHEAD3, BEHIND, LATE = 6, 4, 2, 2, 3
BF16, F32, I32 = jnp.bfloat16, jnp.float32, jnp.int32
HIGH = lax.Precision.HIGHEST
NT = (((1,), (1,)), ((), ()))


def iota(shape, dim):
    return lax.broadcasted_iota(I32, shape, dim)


def kernel(
    x_in, g_in, wg_in, wd_in, pin_in, po_in, st_in, es_ref, bs_ref,
    out,
    wg, wd, xv, gv, st, raw, pin, po, po2, lt, right, pout, rbuf, gat, grouped, place, part, slot,
    lsem, osem, ssem, rsem, sibs, sibr, ysem, yrem, psem, prem, qsem, qrem, tsem, trem,
):
    chunks, tokens = wg.shape[0], xv.shape[0]
    seqs = tokens // SEQ
    s, t = lax.axis_index("store"), lax.axis_index("tensor")
    c, x, z = s % 2, (s // 2) % 4, s // 8

    def dev(zz, xx, cc):
        return (((zz % 4) * 4 + xx % 4) * 2 + cc, t)

    xm, xp, zm, zp = dev(z, x + 3, c), dev(z, x + 1, c), dev(z + 3, x, c), dev(z + 1, x, c)
    sib = dev(z, x, 1 - c)
    ypeer = [(s, (t + i) % 4) for i in (1, 2, 3)]

    barrier = pltpu.get_barrier_semaphore()
    for d in [xm, xp, zm, zp, sib] + ypeer:
        pl.semaphore_signal(barrier, inc=1, device_id=d, device_id_type=MESH)

    copy_raw = pltpu.make_async_copy(wd_in, raw, lsem.at[0])
    copy_raw.start()

    def own_gate(k):
        return pltpu.make_async_copy(
            wg_in.at[:, pl.ds(pl.multiple_of(k * CHUNK, CHUNK), CHUNK)], wg.at[k, c, z, x], osem.at[k]
        )

    for k in range(chunks):
        own_gate(k).start()

    def pieces(n, _):
        cc, hi, lo = n // 16, (n // 4) % 4, n % 4
        to = pl.ds(pl.multiple_of(n * 128, 128), 128)
        a = pl.ds(pl.multiple_of(((hi * 4 + lo) * 2 + cc) * 128, 128), 128)
        b = pl.ds(pl.multiple_of(((lo * 4 + hi) * 2 + cc) * 128, 128), 128)
        pltpu.make_async_copy(x_in.at[:, a], xv.at[:, to], lsem.at[1]).start()
        pltpu.make_async_copy(g_in.at[:, b], gv.at[:, to], lsem.at[2]).start()
        pltpu.make_async_copy(pin_in.at[a], pin.at[to], lsem.at[3]).start()
        return 0

    lax.fori_loop(0, 32, pieces, 0)
    copy_po = pltpu.make_async_copy(po_in, po, lsem.at[4])
    copy_po.start()
    copy_st = pltpu.make_async_copy(st_in, st, lsem.at[5])
    copy_st.start()

    copy_raw.wait()
    for k in range(chunks):
        wd[k, c, x, z] = raw[k * CHUNK : (k + 1) * CHUNK, :].T
    for k in range(chunks):
        own_gate(k).wait()
    pl.semaphore_wait(barrier, 8)

    def sides(ty):
        if ty == 0:
            return wg, z, x, xm, xp, zm, zp
        return wd, x, z, zm, zp, xm, xp

    def rc(ty, k, i, ref, d):
        return pltpu.make_async_remote_copy(
            src_ref=ref, dst_ref=ref, send_sem=ssem.at[ty, i], recv_sem=rsem.at[ty, i, k],
            device_id=d, device_id_type=MESH,
        )

    def msgs(ty, k):
        buf, a, b, bm, bp, am, ap = sides(ty)
        own = buf.at[k, c]
        am1, ap1, ap2 = (a + 3) % 4, (a + 1) % 4, (a + 2) % 4
        bm1, bp1, bp2 = (b + 3) % 4, (b + 1) % 4, (b + 2) % 4
        return (
            [(0, own.at[a, b], bp, own.at[a, bm1]), (1, own.at[a, b], bm, own.at[a, bp1])],
            [
                (2, own.at[a, bm1, 0:64], bp, own.at[a, bp2, 0:64]),
                (3, own.at[a, bp1, 64:128], bm, own.at[a, bp2, 64:128]),
            ],
            [(4, own.at[a], ap, own.at[am1]), (5, own.at[a], am, own.at[ap1])],
            [(6, own.at[am1, 0:2], ap, own.at[ap2, 0:2]), (7, own.at[ap1, 2:4], am, own.at[ap2, 2:4])],
        )

    def start(ty, k, phase):
        for i, ref, d, _ in msgs(ty, k)[phase]:
            rc(ty, k, i, ref, d).start()

    def arrived(ty, k, phase):
        for i, _, d, ref in msgs(ty, k)[phase]:
            rc(ty, k, i, ref, d).wait_recv()

    def shared(ty, k, i):
        buf, a, *_ = sides(ty)
        ref = buf.at[k, c, (a + (0, 3, 1, 2)[i]) % 4]
        return pltpu.make_async_remote_copy(
            src_ref=ref, dst_ref=ref, send_sem=sibs.at[ty, i], recv_sem=sibr.at[ty, k],
            device_id=sib, device_id_type=MESH,
        )

    def from_sibling(ty, k):
        ref = sides(ty)[0].at[k, 1 - c]
        return pltpu.make_async_remote_copy(
            src_ref=ref, dst_ref=ref, send_sem=sibs.at[ty, 0], recv_sem=sibr.at[ty, k],
            device_id=sib, device_id_type=MESH,
        )

    def within(k):
        return jnp.logical_and(k >= 0, k < chunks)

    def transfers(j):
        @pl.when(within(j + AHEAD1))
        def _():
            for ty in range(2):
                start(ty, j + AHEAD1, 0)

        @pl.when(within(j + AHEAD2))
        def _():
            for ty in range(2):
                arrived(ty, j + AHEAD2, 0)
                start(ty, j + AHEAD2, 1)

        @pl.when(within(j + AHEAD3))
        def _():
            for ty in range(2):
                arrived(ty, j + AHEAD3, 1)
                start(ty, j + AHEAD3, 2)
                shared(ty, j + AHEAD3, 0).start()

        @pl.when(within(j))
        def _():
            for ty in range(2):
                arrived(ty, j, 2)
                start(ty, j, 3)
                shared(ty, j, 1).start()
                shared(ty, j, 2).start()

        @pl.when(within(j - BEHIND))
        def _():
            for ty in range(2):
                arrived(ty, j - BEHIND, 3)
                shared(ty, j - BEHIND, 3).start()

    def hidden(k):
        for ty in range(2):
            from_sibling(ty, k).wait_recv()
        proj = po2[pl.ds(pl.multiple_of(k * CHUNK, CHUNK), CHUNK), :]

        def rows(m, _):
            at = pl.ds(pl.multiple_of(m * 256, 256), 256)
            gate = jnp.dot(xv[at, :], wg[k].reshape(4096, CHUNK), preferred_element_type=F32)
            back = jnp.dot(gv[at, :], wd[k].reshape(4096, CHUNK), preferred_element_type=F32)
            update = (back * (gate / (1.0 + jnp.exp(-gate)))).astype(BF16)
            right[at, :] += jnp.dot(update, proj, preferred_element_type=F32)
            return 0

        lax.fori_loop(0, tokens // 256, rows, 0)

    def before(j, _):
        transfers(j)
        return 0

    lax.fori_loop(-AHEAD1, 0, before, 0)

    right[...] = jnp.zeros_like(right)
    row = es_ref[...]
    col = jnp.sum(jnp.where(iota((192, 192), 0) == iota((192, 192), 1), row, 0), axis=1, keepdims=True)
    pos = iota((192, 256), 1)
    n, q = pos // 8, pos % 8
    ev = ((((n // 4) % 4) * 4 + n % 4) * 2 + n // 16) * 6 + q
    pick = jnp.logical_and(ev == iota((192, 256), 0), q < 6)
    stratum = jnp.sum(jnp.where(pick, col + 1, 0), axis=0, keepdims=True) - 1
    same = jnp.logical_and(row == col, iota((192, 192), 0) < iota((192, 192), 1))
    rank = jnp.sum(same.astype(I32), axis=0, keepdims=True)
    rank_col = jnp.sum(jnp.where(iota((192, 192), 0) == iota((192, 192), 1), rank, 0), axis=1, keepdims=True)
    slot[...] = col * PAD + rank_col
    target = jnp.sum(jnp.where(pick, col * PAD + rank_col, 0), axis=0, keepdims=True)
    target = jnp.where(stratum >= 0, target, -1)
    place[...] = (iota((256, 256), 0) == target).astype(F32).astype(BF16)
    copy_po.wait()
    po2[...] = jnp.concatenate([po[...], po[...]], axis=1)
    pltpu.make_async_copy(x_in, xv, lsem.at[1]).wait()
    pltpu.make_async_copy(pin_in, pin, lsem.at[3]).wait()
    halves = iota((64, 64), 1)
    order = (iota((64, 64), 0) == jnp.where(halves < 32, 2 * halves, 2 * halves - 63)).astype(F32)

    def left_rows(m, _):
        at = pl.ds(pl.multiple_of(m * SEQ, SEQ), SEQ)
        left = jnp.dot(xv[at, :], pin[...], preferred_element_type=F32)
        left = jnp.dot(left, order, precision=HIGH, preferred_element_type=F32)
        lt[m] = left.T
        return 0

    lax.fori_loop(0, seqs, left_rows, 0)
    pltpu.make_async_copy(g_in, gv, lsem.at[2]).wait()
    copy_st.wait()

    def steady(j, _):
        transfers(j)

        @pl.when(within(j - LATE))
        def _():
            hidden(j - LATE)

        return 0

    lax.fori_loop(0, chunks + LATE, steady, 0)

    lane = iota((32, 128), 1)
    for m in range(seqs):
        both = jnp.dot(lt[m], right[m * SEQ : (m + 1) * SEQ, :], precision=HIGH, preferred_element_type=F32)
        flat = jnp.where(lane < 64, both[0:32], both[32:64])
        for u in range(4):
            pout[u, m] = flat[u * 8 : u * 8 + 8]

    def quarter(i, to, at):
        return pltpu.make_async_remote_copy(
            src_ref=pout.at[to], dst_ref=rbuf.at[at], send_sem=ysem.at[i], recv_sem=yrem.at[i],
            device_id=(s, to), device_id_type=MESH,
        )

    for i in range(3):
        quarter(i, (t + i + 1) % 4, t).start()
    total = pout[t]
    for i in range(3):
        quarter(i, (t + i + 1) % 4, (t + 3 - i) % 4).wait_recv()
        total += rbuf[(t + 3 - i) % 4]
    mine = (total * (1.0 / SEQ)).reshape(seqs * 8, 128).astype(BF16)
    to, fr = iota((64, 48), 0), iota((64, 48), 1)
    turn = jnp.logical_and(fr // 8 == to % 8, fr % 8 == to // 8).astype(F32).astype(BF16)
    gat[c, z, x] = jnp.dot(turn, mine, preferred_element_type=F32).astype(BF16)

    def flat_copy(i, zz, xx):
        return pltpu.make_async_remote_copy(
            src_ref=gat.at[c, zz, xx], dst_ref=gat.at[c, zz, xx], send_sem=psem.at[i], recv_sem=prem.at[i],
            device_id=dev(z + i // 4, x + i % 4, c), device_id_type=MESH,
        )

    for i in (10, 6, 14, 9, 11, 2, 8, 5, 7, 13, 15, 1, 3, 4, 12):
        flat_copy(i, z, x).start()
    for i in (1, 3, 4, 12, 5, 7, 13, 15, 2, 8, 6, 14, 9, 11, 10):
        flat_copy(i, (z + 4 - i // 4) % 4, (x + 4 - i % 4) % 4).wait_recv()

    def flat_shared(cc):
        return pltpu.make_async_remote_copy(
            src_ref=gat.at[cc], dst_ref=gat.at[cc], send_sem=tsem, recv_sem=trem,
            device_id=sib, device_id_type=MESH,
        )

    flat_shared(c).start()
    flat_shared(1 - c).wait_recv()
    flats = gat[...].reshape(32, 64, 128).astype(F32)
    for kk in range(8):
        some = flats[:, kk * 8 : kk * 8 + 8, :].reshape(256, 128).astype(BF16)
        rows = jnp.dot(place[...], some, preferred_element_type=F32).astype(BF16)
        grouped[:, :, kk * 128 : (kk + 1) * 128] = rows.reshape(STRATA, PAD, 128)

    def part_copy(g, i, to, at):
        ref = part.at[at, pl.ds(g * 4, 4)]
        return pltpu.make_async_remote_copy(
            src_ref=ref, dst_ref=ref, send_sem=qsem.at[g, i], recv_sem=qrem.at[g, i],
            device_id=(s, to), device_id_type=MESH,
        )

    def group(g, _):
        def pair(p, _):
            m = g * 4 + p
            two = []
            for e in range(2):
                b = 2 * m + e
                stored = st[pl.ds(pl.multiple_of(b * BLOCK, BLOCK), BLOCK), :]
                chosen = grouped[bs_ref[b]]
                two.append(lax.dot_general(chosen, stored, NT, preferred_element_type=F32)[0:PER])
            part[t, m] = jnp.concatenate(two, axis=0).astype(BF16)
            return 0

        lax.fori_loop(0, 4, pair, 0)
        for i in range(3):
            part_copy(g, i, (t + i + 1) % 4, t).start()
        return 0

    lax.fori_loop(0, 4, group, 0)

    own = slot[pl.ds(pl.multiple_of(t * 48, 8), 48), :]
    own = jnp.concatenate([own, own], axis=0)
    half = iota((96, 192), 0) // 48
    entry = iota((96, 192), 1) % 48
    block_of, rank_of = entry // PER, entry % PER

    def expand(g, _):
        for i in range(3):
            part_copy(g, i, (t + i + 1) % 4, (t + 3 - i) % 4).wait_recv()

        def pair(p, _):
            m = g * 4 + p
            strata = jnp.where(block_of == 0, bs_ref[2 * m], bs_ref[2 * m + 1])
            chosen = jnp.logical_and(own == strata * PAD + rank_of, half == block_of)
            summed = jnp.dot(
                chosen.astype(F32).astype(BF16), part[:, m].reshape(192, 128), preferred_element_type=F32
            )
            out[:, pl.ds(pl.multiple_of(m * 256, 256), 256)] = jnp.concatenate([summed[0:48], summed[48:96]], axis=1)
            return 0

        lax.fori_loop(0, 4, pair, 0)
        return 0

    lax.fori_loop(0, 4, expand, 0)

    for ty in range(2):
        buf, a, b, bm, bp, am, ap = sides(ty)
        own_buf = buf.at[:, c]
        sizes = [
            own_buf.at[:, a, b], own_buf.at[:, a, b], own_buf.at[:, a, b, 0:64], own_buf.at[:, a, b, 0:64],
            own_buf.at[:, a], own_buf.at[:, a], own_buf.at[:, a, 0:2], own_buf.at[:, a, 0:2],
        ]
        for i, ref in enumerate(sizes):
            rc(ty, 0, i, ref, xm).wait_send()
        for i in range(4):
            ref = own_buf.at[:, a]
            pltpu.make_async_remote_copy(
                src_ref=ref, dst_ref=ref, send_sem=sibs.at[ty, i], recv_sem=sibr.at[ty, 0],
                device_id=sib, device_id_type=MESH,
            ).wait_send()
    for i in range(3):
        quarter(i, (t + i + 1) % 4, t).wait_send()
    for i in range(1, 16):
        flat_copy(i, z, x).wait_send()
    flat_shared(c).wait_send()
    for g in range(4):
        for i in range(3):
            part_copy(g, i, (t + i + 1) % 4, t).wait_send()


def local(eval_inputs, eval_grads, w_gate, w_down, proj_in, proj_out, store_rows, eval_strata, block_strata):
    tokens, width = eval_inputs.shape
    cols = w_gate.shape[1]
    chunks = cols // CHUNK
    rows, feats = store_rows.shape
    any_space = pl.BlockSpec(memory_space=pl.ANY)
    dma = pltpu.SemaphoreType.DMA
    evals = eval_strata.shape[0]
    seqs = tokens // SEQ
    return pl.pallas_call(
        kernel,
        out_shape=jax.ShapeDtypeStruct((evals // 4, rows), F32),
        in_specs=[any_space] * 7
        + [pl.BlockSpec(memory_space=pltpu.VMEM), pl.BlockSpec(memory_space=pltpu.SMEM)],
        out_specs=pl.BlockSpec(memory_space=pltpu.VMEM),
        scratch_shapes=[
            pltpu.VMEM((chunks, 2, 4, 4, 128, CHUNK), BF16),
            pltpu.VMEM((chunks, 2, 4, 4, 128, CHUNK), BF16),
            pltpu.VMEM((tokens, width), BF16),
            pltpu.VMEM((tokens, width), BF16),
            pltpu.VMEM((rows, feats), BF16),
            pltpu.VMEM((cols, 128), BF16),
            pltpu.VMEM((width, RANK), BF16),
            pltpu.VMEM((cols, RANK), BF16),
            pltpu.VMEM((cols, 2 * RANK), BF16),
            pltpu.VMEM((seqs, RANK, SEQ), F32),
            pltpu.VMEM((tokens, 2 * RANK), F32),
            pltpu.VMEM((4, seqs, 8, 128), F32),
            pltpu.VMEM((4, seqs, 8, 128), F32),
            pltpu.VMEM((2, 4, 4, 64, 128), BF16),
            pltpu.VMEM((STRATA, PAD, feats), BF16),
            pltpu.VMEM((256, 256), BF16),
            pltpu.VMEM((4, rows // (2 * BLOCK), 2 * PER, BLOCK), BF16),
            pltpu.VMEM((evals, 1), I32),
            dma((6,)),
            dma((chunks,)),
            dma((2, 8)),
            dma((2, 8, chunks)),
            dma((2, 4)),
            dma((2, chunks)),
            dma((3,)),
            dma((3,)),
            dma((16,)),
            dma((16,)),
            dma((4, 3)),
            dma((4, 3)),
            dma,
            dma,
        ],
        compiler_params=pltpu.CompilerParams(
            collective_id=0, has_side_effects=True, vmem_limit_bytes=64 * 2**20 - 2**19
        ),
    )(
        eval_inputs, eval_grads, w_gate, w_down, proj_in, proj_out, store_rows,
        eval_strata.reshape(1, evals), block_strata,
    )


def solution(mesh):
    return jax.shard_map(
        local,
        mesh=mesh,
        in_specs=(
            P("store", None),
            P("store", None),
            P("store", "tensor"),
            P("tensor", "store"),
            P(),
            P("tensor", None),
            P("store", "tensor"),
            P(),
            P("store"),
        ),
        out_specs=P("tensor", "store"),
        check_vma=False,
    )
```

```python
import functools

import jax
import jax.numpy as jnp
from jax import lax
from jax.experimental import pallas as pl
from jax.experimental.pallas import tpu as pltpu
from jax.sharding import PartitionSpec as P

MESH = pl.DeviceIdType.MESH
RANK, SEQ, BLOCK, STRATA = 64, 128, 128, 8
PAD = 32
CHUNK = 256
AHEAD1, AHEAD2, AHEAD3 = 6, 4, 2
ORDER = "edrabRcmM"
TILE = 384
BF16, F32, I32 = jnp.bfloat16, jnp.float32, jnp.int32
HIGH = lax.Precision.HIGHEST
NT = (((1,), (1,)), ((), ()))


def iota(shape, dim):
    return lax.broadcasted_iota(I32, shape, dim)


def kernel(
    x_in, g_in, wg_in, wd_in, pin_in, po_in, st_in, es_ref, bs_ref,
    out,
    wg, wd, xv, gv, st, raw, pin, po, po2, lt, acc, right, pout, rbuf, gat, grouped, place, part, got, full, slot,
    lsem, osem, ssem, rsem, sibs, sibr, ysem, yrem, psem, prem, qsem, qrem, fsem, frem, tsem, trem,
):
    chunks, tokens = wg.shape[0], xv.shape[0]
    seqs = tokens // SEQ
    s, t = lax.axis_index("store"), lax.axis_index("tensor")
    c, x, z = s % 2, (s // 2) % 4, s // 8

    def dev(zz, xx, cc):
        return (((zz % 4) * 4 + xx % 4) * 2 + cc, t)

    xm, xp, zm, zp = dev(z, x + 3, c), dev(z, x + 1, c), dev(z + 3, x, c), dev(z + 1, x, c)
    sib = dev(z, x, 1 - c)
    ypeer = [(s, (t + i) % 4) for i in (1, 2, 3)]

    barrier = pltpu.get_barrier_semaphore()
    for d in [xm, xp, zm, zp, sib] + ypeer:
        pl.semaphore_signal(barrier, inc=1, device_id=d, device_id_type=MESH)

    copy_raw = pltpu.make_async_copy(wd_in, raw, lsem.at[0])
    copy_raw.start()

    def own_gate(k):
        return pltpu.make_async_copy(
            wg_in.at[:, pl.ds(pl.multiple_of(k * CHUNK, CHUNK), CHUNK)], wg.at[k, c, z, x], osem.at[k]
        )

    for k in range(chunks):
        own_gate(k).start()

    copy_raw.wait()
    for k in range(chunks):
        wd[k, c, x, z] = raw[k * CHUNK : (k + 1) * CHUNK, :].T
    for k in range(chunks):
        own_gate(k).wait()
    pl.semaphore_wait(barrier, 8)

    def pieces(n, _):
        cc, hi, lo = n // 16, (n // 4) % 4, n % 4
        to = pl.ds(pl.multiple_of(n * 128, 128), 128)
        a = pl.ds(pl.multiple_of(((hi * 4 + lo) * 2 + cc) * 128, 128), 128)
        b = pl.ds(pl.multiple_of(((lo * 4 + hi) * 2 + cc) * 128, 128), 128)
        pltpu.make_async_copy(x_in.at[:, a], xv.at[:, to], lsem.at[1]).start()
        pltpu.make_async_copy(g_in.at[:, b], gv.at[:, to], lsem.at[2]).start()
        pltpu.make_async_copy(pin_in.at[:, a], pin.at[:, to], lsem.at[3]).start()
        return 0

    copy_po = pltpu.make_async_copy(po_in, po, lsem.at[4])
    copy_st = pltpu.make_async_copy(st_in, st, lsem.at[5])

    def loads():
        copy_po.start()
        lax.fori_loop(0, 32, pieces, 0)
        copy_st.start()

    def sides(ty):
        if ty == 0:
            return wg, z, x, xm, xp, zm, zp
        return wd, x, z, zm, zp, xm, xp

    def rc(ty, k, i, ref, d):
        return pltpu.make_async_remote_copy(
            src_ref=ref, dst_ref=ref, send_sem=ssem.at[ty, i], recv_sem=rsem.at[ty, i, k],
            device_id=d, device_id_type=MESH,
        )

    def msgs(ty, k):
        buf, a, b, bm, bp, am, ap = sides(ty)
        own = buf.at[k, c]
        am1, ap1, ap2 = (a + 3) % 4, (a + 1) % 4, (a + 2) % 4
        bm1, bp1, bp2 = (b + 3) % 4, (b + 1) % 4, (b + 2) % 4
        return (
            [(0, own.at[a, b], bp, own.at[a, bm1]), (1, own.at[a, b], bm, own.at[a, bp1])],
            [
                (2, own.at[a, bm1, 0:64], bp, own.at[a, bp2, 0:64]),
                (3, own.at[a, bp1, 64:128], bm, own.at[a, bp2, 64:128]),
            ],
            [(4, own.at[a], ap, own.at[am1]), (5, own.at[a], am, own.at[ap1])],
            [(6, own.at[am1, 0:2], ap, own.at[ap2, 0:2]), (7, own.at[ap1, 2:4], am, own.at[ap2, 2:4])],
        )

    def start(ty, k, phase):
        for i, ref, d, _ in msgs(ty, k)[phase]:
            rc(ty, k, i, ref, d).start()

    def arrived(ty, k, phase):
        for i, _, d, ref in msgs(ty, k)[phase]:
            rc(ty, k, i, ref, d).wait_recv()

    def shared(ty, k, i):
        buf, a, *_ = sides(ty)
        ref = buf.at[k, c, (a + (0, 3, 1, 2)[i]) % 4]
        return pltpu.make_async_remote_copy(
            src_ref=ref, dst_ref=ref, send_sem=sibs.at[ty, i], recv_sem=sibr.at[ty, i // 3, k],
            device_id=sib, device_id_type=MESH,
        )

    def from_sibling(ty, k, last):
        ref = sides(ty)[0].at[k, 1 - c, 3:4] if last else sides(ty)[0].at[k, 1 - c, 0:3]
        return pltpu.make_async_remote_copy(
            src_ref=ref, dst_ref=ref, send_sem=sibs.at[ty, 0], recv_sem=sibr.at[ty, last, k],
            device_id=sib, device_id_type=MESH,
        )

    def within(k):
        if isinstance(k, int):
            return lambda f: f() if 0 <= k < chunks else None
        return pl.when(jnp.logical_and(k >= 0, k < chunks))

    def first_hop(j):
        @within(j + AHEAD1)
        def _():
            for ty in range(2):
                start(ty, j + AHEAD1, 0)

    def second_hop(j):
        @within(j + AHEAD2)
        def _():
            for ty in range(2):
                arrived(ty, j + AHEAD2, 0)
                start(ty, j + AHEAD2, 1)

    def third_hop(j):
        @within(j + AHEAD3)
        def _():
            for ty in range(2):
                arrived(ty, j + AHEAD3, 1)
                start(ty, j + AHEAD3, 2)
                shared(ty, j + AHEAD3, 0).start()

    def fourth_hop(j):
        @within(j)
        def _():
            for ty in range(2):
                arrived(ty, j, 2)
                start(ty, j, 3)
                shared(ty, j, 1).start()
                shared(ty, j, 2).start()

    def last_line(j):
        @within(j - 1)
        def _():
            for ty in range(2):
                arrived(ty, j - 1, 3)
                shared(ty, j - 1, 3).start()

    def product(at, ty, k, lines):
        lhs, rhs = (xv, wg) if ty == 0 else (gv, wd)
        total = None
        for line in lines:
            for cc in range(2):
                cols = pl.ds(pl.multiple_of((cc * 4 + line) * 512, 512), 512)
                term = jnp.dot(lhs[at, cols], rhs[k, cc, line].reshape(512, CHUNK), preferred_element_type=F32)
                total = term if total is None else total + term
        return total

    def most(j, part):
        @within(j)
        def _():
            at = pl.ds(part * TILE, TILE)
            for ty in range(2):
                if part == 0:
                    from_sibling(ty, j, 0).wait_recv()
            for ty in range(2):
                a = (z, x)[ty]
                acc[ty, at, :] = product(at, ty, j, [a, (a + 1) % 4, (a + 3) % 4])

    def rest(j, part):
        @within(j - 1)
        def _():
            k = j - 1
            at = pl.ds(part * TILE, TILE)
            for ty in range(2):
                if part == 0:
                    from_sibling(ty, k, 1).wait_recv()
            proj = po2[pl.ds(pl.multiple_of(k * CHUNK, CHUNK), CHUNK), :]
            gate = acc[0, at, :] + product(at, 0, k, [(z + 2) % 4])
            back = acc[1, at, :] + product(at, 1, k, [(x + 2) % 4])
            update = (back * (gate / (1.0 + jnp.exp(-gate)))).astype(BF16)
            right[at, :] += jnp.dot(update, proj, preferred_element_type=F32)

    def tables():
        row = es_ref[...]
        diag = iota((192, 192), 0) == iota((192, 192), 1)
        col = jnp.sum(jnp.where(diag, row, 0), axis=1, keepdims=True)
        same = jnp.logical_and(row == col, iota((192, 192), 0) < iota((192, 192), 1))
        rank = jnp.sum(same.astype(I32), axis=0, keepdims=True)
        rank = jnp.sum(jnp.where(diag, rank, 0), axis=1, keepdims=True)
        here = col * PAD + (rank // 6) * 8 + rank % 6
        slot[...] = here
        pos = iota((192, 256), 1)
        n, q = pos // 8, pos % 8
        ev = ((((n // 4) % 4) * 4 + n % 4) * 2 + n // 16) * 6 + q
        pick = jnp.logical_and(ev == iota((192, 256), 0), q < 6)
        target = jnp.sum(jnp.where(pick, here + 1, 0), axis=0, keepdims=True) - 1
        place[...] = (iota((256, 256), 0) == target).astype(F32).astype(BF16)

    def projections():
        right[...] = jnp.zeros_like(right)
        copy_po.wait()
        side = po[...].T
        po2[...] = jnp.concatenate([side, side], axis=1)
        pltpu.make_async_copy(x_in, xv, lsem.at[1]).wait()
        pltpu.make_async_copy(pin_in, pin, lsem.at[3]).wait()
        to = iota((64, 64), 0)
        order = (iota((64, 64), 1) == jnp.where(to < 32, 2 * to, 2 * to - 63)).astype(F32).astype(BF16)
        pin[...] = jnp.dot(order, pin[...], preferred_element_type=F32).astype(BF16)

    def lefts(m):
        lt[m] = lax.dot_general(pin[...], xv[m * SEQ : (m + 1) * SEQ, :], NT, preferred_element_type=F32)

    work = {
        0: [loads],
        1: [tables],
        2: [projections],
    }
    for m in range(seqs):
        work.setdefault(3 + m // 2, []).append(functools.partial(lefts, m))
    for j in range(AHEAD1):
        for f in (first_hop, second_hop, third_hop):
            f(j - AHEAD1)
        for f in work.get(j, []):
            f()
    pltpu.make_async_copy(g_in, gv, lsem.at[2]).wait()
    copy_st.wait()

    steps = {
        "a": first_hop, "b": second_hop, "c": third_hop, "d": fourth_hop, "e": last_line,
        "m": functools.partial(most, part=0), "M": functools.partial(most, part=1),
        "r": functools.partial(rest, part=0), "R": functools.partial(rest, part=1),
    }

    def steady(j, _):
        for name in ORDER:
            steps[name](j)
        return 0

    lax.fori_loop(0, chunks + 1, steady, 0)

    lane = iota((32, 128), 1)
    for m in range(seqs):
        both = jnp.dot(lt[m], right[m * SEQ : (m + 1) * SEQ, :], precision=HIGH, preferred_element_type=F32)
        flat = jnp.where(lane < 64, both[0:32], both[32:64])
        for u in range(4):
            pout[u, m] = flat[u * 8 : u * 8 + 8]

    def quarter(i, to, at):
        return pltpu.make_async_remote_copy(
            src_ref=pout.at[to], dst_ref=rbuf.at[at], send_sem=ysem.at[i], recv_sem=yrem.at[i],
            device_id=(s, to), device_id_type=MESH,
        )

    for i in range(3):
        quarter(i, (t + i + 1) % 4, t).start()
    total = pout[t]
    for i in range(3):
        quarter(i, (t + i + 1) % 4, (t + 3 - i) % 4).wait_recv()
        total += rbuf[(t + 3 - i) % 4]
    mine = (total * (1.0 / SEQ)).reshape(seqs * 8, 128).astype(BF16)
    to, fr = iota((64, 48), 0), iota((64, 48), 1)
    turn = jnp.logical_and(fr // 8 == to % 8, fr % 8 == to // 8).astype(F32).astype(BF16)
    gat[c, z, x] = jnp.dot(turn, mine, preferred_element_type=F32).astype(BF16)

    def flat_copy(i, zz, xx):
        return pltpu.make_async_remote_copy(
            src_ref=gat.at[c, zz, xx], dst_ref=gat.at[c, zz, xx], send_sem=psem.at[i], recv_sem=prem.at[i],
            device_id=dev(z + i // 4, x + i % 4, c), device_id_type=MESH,
        )

    for i in (10, 6, 14, 9, 11, 2, 8, 5, 7, 13, 15, 1, 3, 4, 12):
        flat_copy(i, z, x).start()

    def flat_shared(ref):
        return pltpu.make_async_remote_copy(
            src_ref=ref, dst_ref=ref, send_sem=tsem, recv_sem=trem, device_id=sib, device_id_type=MESH
        )

    flat_shared(gat.at[c, z, x]).start()
    for i in (1, 3, 4, 12, 5, 7, 13, 15, 2, 8, 6, 14, 9, 11, 10):
        zz, xx = (z + 4 - i // 4) % 4, (x + 4 - i % 4) % 4
        flat_copy(i, zz, xx).wait_recv()
        flat_shared(gat.at[c, zz, xx]).start()
    flat_shared(gat.at[1 - c]).wait_recv()
    flats = gat[...].reshape(32, 64, 128).astype(F32)
    for kk in range(8):
        some = flats[:, kk * 8 : kk * 8 + 8, :].reshape(256, 128).astype(BF16)
        rows = jnp.dot(place[...], some, preferred_element_type=F32).astype(BF16)
        grouped[:, :, kk * 128 : (kk + 1) * 128] = rows.reshape(STRATA, PAD, 128)

    def part_copy(g, i, to, at):
        some = pl.ds(g * 8, 8)
        return pltpu.make_async_remote_copy(
            src_ref=part.at[to, some], dst_ref=got.at[at, some], send_sem=qsem.at[g, i], recv_sem=qrem.at[g, i],
            device_id=(s, to), device_id_type=MESH,
        )

    def full_copy(g, i, to, at):
        ref = full.at[at, pl.ds(g * 8, 8)]
        return pltpu.make_async_remote_copy(
            src_ref=ref, dst_ref=ref, send_sem=fsem.at[g, i], recv_sem=frem.at[g, i],
            device_id=(s, to), device_id_type=MESH,
        )

    for g in range(2):

        def blocks(p, _):
            first = g * 8 + p * 4
            found = []
            for e in range(8):
                b = 2 * first + e
                stored = st[pl.ds(pl.multiple_of(b * BLOCK, BLOCK), BLOCK), :]
                found.append(lax.dot_general(grouped[bs_ref[b]], stored, NT, preferred_element_type=F32))
            for m in range(4):
                for u in range(4):
                    both = [r[u * 8 : u * 8 + 8] for r in found[2 * m : 2 * m + 2]]
                    part[u, first + m] = jnp.concatenate(both, axis=0).astype(BF16)
            return 0

        lax.fori_loop(0, 2, blocks, 0)
        for i in range(3):
            part_copy(g, i, (t + i + 1) % 4, t).start()
    for g in range(2):
        for i in range(3):
            part_copy(g, i, (t + i + 1) % 4, (t + 3 - i) % 4).wait_recv()
        some = pl.ds(g * 8, 8)
        total = part[t, some].astype(F32)
        for i in range(3):
            total += got[(t + 3 - i) % 4, some].astype(F32)
        full[t, some] = total.astype(BF16)
        for i in range(3):
            full_copy(g, i, (t + i + 1) % 4, t).start()

    own = slot[pl.ds(pl.multiple_of(t * 48, 8), 48), :]
    entry = iota((96, 64), 1)
    block_of = (entry // 8) % 2
    rest_of = jnp.concatenate([own, own], axis=0) - (entry // 16) * 8 - entry % 8
    rest_of = jnp.where(iota((96, 64), 0) // 48 == block_of, rest_of, -1)
    for g in range(2):
        for i in range(3):
            full_copy(g, i, (t + i + 1) % 4, (t + 3 - i) % 4).wait_recv()

        def expand(p, _):
            for e in range(4):
                m = g * 8 + p * 4 + e
                chosen = rest_of == jnp.where(block_of == 0, bs_ref[2 * m] * PAD, bs_ref[2 * m + 1] * PAD)
                summed = jnp.dot(
                    chosen.astype(F32).astype(BF16), full[:, m].reshape(64, 128), preferred_element_type=F32
                )
                at = pl.multiple_of(m * 2 * BLOCK, 2 * BLOCK)
                out[:, pl.ds(at, BLOCK)] = summed[0:48]
                out[:, pl.ds(at + BLOCK, BLOCK)] = summed[48:96]
            return 0

        lax.fori_loop(0, 2, expand, 0)

    for ty in range(2):
        buf, a, b, bm, bp, am, ap = sides(ty)
        own_buf = buf.at[:, c]
        sizes = [
            own_buf.at[:, a, b], own_buf.at[:, a, b], own_buf.at[:, a, b, 0:64], own_buf.at[:, a, b, 0:64],
            own_buf.at[:, a], own_buf.at[:, a], own_buf.at[:, a, 0:2], own_buf.at[:, a, 0:2],
        ]
        for i, ref in enumerate(sizes):
            rc(ty, 0, i, ref, xm).wait_send()
        for i in range(4):
            ref = own_buf.at[:, a]
            pltpu.make_async_remote_copy(
                src_ref=ref, dst_ref=ref, send_sem=sibs.at[ty, i], recv_sem=sibr.at[ty, 0, 0],
                device_id=sib, device_id_type=MESH,
            ).wait_send()
    for i in range(3):
        quarter(i, (t + i + 1) % 4, t).wait_send()
    for i in range(1, 16):
        flat_copy(i, z, x).wait_send()
    flat_shared(gat.at[c]).wait_send()
    for g in range(2):
        for i in range(3):
            part_copy(g, i, (t + i + 1) % 4, t).wait_send()
            full_copy(g, i, (t + i + 1) % 4, t).wait_send()


def local(eval_inputs, eval_grads, w_gate, w_down, proj_in, proj_out, store_rows, eval_strata, block_strata):
    tokens, width = eval_inputs.shape
    cols = w_gate.shape[1]
    chunks = cols // CHUNK
    rows, feats = store_rows.shape
    any_space = pl.BlockSpec(memory_space=pl.ANY)
    dma = pltpu.SemaphoreType.DMA
    evals = eval_strata.shape[0]
    seqs = tokens // SEQ
    return pl.pallas_call(
        kernel,
        out_shape=jax.ShapeDtypeStruct((evals // 4, rows), F32),
        in_specs=[any_space] * 7
        + [pl.BlockSpec(memory_space=pltpu.VMEM), pl.BlockSpec(memory_space=pltpu.SMEM)],
        out_specs=pl.BlockSpec(memory_space=pltpu.VMEM),
        scratch_shapes=[
            pltpu.VMEM((chunks, 2, 4, 4, 128, CHUNK), BF16),
            pltpu.VMEM((chunks, 2, 4, 4, 128, CHUNK), BF16),
            pltpu.VMEM((tokens, width), BF16),
            pltpu.VMEM((tokens, width), BF16),
            pltpu.VMEM((rows, feats), BF16),
            pltpu.VMEM((cols, 128), BF16),
            pltpu.VMEM((RANK, width), BF16),
            pltpu.VMEM((RANK, cols), BF16),
            pltpu.VMEM((cols, 2 * RANK), BF16),
            pltpu.VMEM((seqs, RANK, SEQ), F32),
            pltpu.VMEM((2, tokens, CHUNK), F32),
            pltpu.VMEM((tokens, 2 * RANK), F32),
            pltpu.VMEM((4, seqs, 8, 128), F32),
            pltpu.VMEM((4, seqs, 8, 128), F32),
            pltpu.VMEM((2, 4, 4, 64, 128), BF16),
            pltpu.VMEM((STRATA, PAD, feats), BF16),
            pltpu.VMEM((256, 256), BF16),
            pltpu.VMEM((4, rows // (2 * BLOCK), 16, BLOCK), BF16),
            pltpu.VMEM((4, rows // (2 * BLOCK), 16, BLOCK), BF16),
            pltpu.VMEM((4, rows // (2 * BLOCK), 16, BLOCK), BF16),
            pltpu.VMEM((evals, 1), I32),
            dma((6,)),
            dma((chunks,)),
            dma((2, 8)),
            dma((2, 8, chunks)),
            dma((2, 4)),
            dma((2, 2, chunks)),
            dma((3,)),
            dma((3,)),
            dma((16,)),
            dma((16,)),
            dma((2, 3)),
            dma((2, 3)),
            dma((2, 3)),
            dma((2, 3)),
            dma,
            dma,
        ],
        compiler_params=pltpu.CompilerParams(
            collective_id=0, has_side_effects=True, vmem_limit_bytes=57 * 2**20
        ),
    )(
        eval_inputs, eval_grads, w_gate, w_down, proj_in.T, proj_out.T, store_rows,
        eval_strata.reshape(1, evals), block_strata,
    )


def solution(mesh):
    return jax.shard_map(
        local,
        mesh=mesh,
        in_specs=(
            P("store", None),
            P("store", None),
            P("store", "tensor"),
            P("tensor", "store"),
            P(),
            P("tensor", None),
            P("store", "tensor"),
            P(),
            P("store"),
        ),
        out_specs=P("tensor", "store"),
        check_vma=False,
    )
```

```python
import functools

import jax
import jax.numpy as jnp
from jax import lax
from jax.experimental import pallas as pl
from jax.experimental.pallas import tpu as pltpu
from jax.sharding import PartitionSpec as P

MESH = pl.DeviceIdType.MESH
RANK, SEQ, BLOCK, STRATA = 64, 128, 128, 8
PAD = 32
CHUNK = 256
AHEAD1, AHEAD2, AHEAD3 = 6, 4, 2
ORDER = "edrabRcmM"
TILE = 384
BF16, F32, I32 = jnp.bfloat16, jnp.float32, jnp.int32
HIGH = lax.Precision.HIGHEST
NT = (((1,), (1,)), ((), ()))


def iota(shape, dim):
    return lax.broadcasted_iota(I32, shape, dim)


def kernel(
    x_in, g_in, wg_in, wd_in, pin_in, po_in, st_in, es_ref, bs_ref,
    out,
    wg, wd, xv, gv, st, raw, pin, po, po2, lt, acc, right, pout, rbuf, gat, grouped, place, part, got, full, slot,
    lsem, osem, ssem, rsem, sibs, sibr, ysem, yrem, psem, prem, qsem, qrem, fsem, frem, tsem, trem,
):
    chunks, tokens = wg.shape[0], xv.shape[0]
    seqs = tokens // SEQ
    s, t = lax.axis_index("store"), lax.axis_index("tensor")
    c, x, z = s % 2, (s // 2) % 4, s // 8

    def dev(zz, xx, cc):
        return (((zz % 4) * 4 + xx % 4) * 2 + cc, t)

    xm, xp, zm, zp = dev(z, x + 3, c), dev(z, x + 1, c), dev(z + 3, x, c), dev(z + 1, x, c)
    sib = dev(z, x, 1 - c)
    ypeer = [(s, (t + i) % 4) for i in (1, 2, 3)]

    barrier = pltpu.get_barrier_semaphore()
    for d in [xm, xp, zm, zp, sib] + ypeer:
        pl.semaphore_signal(barrier, inc=1, device_id=d, device_id_type=MESH)

    copy_raw = pltpu.make_async_copy(wd_in, raw, lsem.at[0])
    copy_raw.start()

    def own_gate(k):
        return pltpu.make_async_copy(
            wg_in.at[:, pl.ds(pl.multiple_of(k * CHUNK, CHUNK), CHUNK)], wg.at[k, c, z, x], osem.at[k]
        )

    for k in range(chunks):
        own_gate(k).start()

    copy_raw.wait()
    for k in range(chunks):
        wd[k, c, x, z] = raw[k * CHUNK : (k + 1) * CHUNK, :].T
    for k in range(chunks):
        own_gate(k).wait()
    pl.semaphore_wait(barrier, 8)

    def pieces(n, _):
        cc, hi, lo = n // 16, (n // 4) % 4, n % 4
        to = pl.ds(pl.multiple_of(n * 128, 128), 128)
        a = pl.ds(pl.multiple_of(((hi * 4 + lo) * 2 + cc) * 128, 128), 128)
        b = pl.ds(pl.multiple_of(((lo * 4 + hi) * 2 + cc) * 128, 128), 128)
        pltpu.make_async_copy(x_in.at[:, a], xv.at[:, to], lsem.at[1]).start()
        pltpu.make_async_copy(g_in.at[:, b], gv.at[:, to], lsem.at[2]).start()
        pltpu.make_async_copy(pin_in.at[:, a], pin.at[:, to], lsem.at[3]).start()
        return 0

    copy_po = pltpu.make_async_copy(po_in, po, lsem.at[4])
    copy_st = pltpu.make_async_copy(st_in, st, lsem.at[5])

    def loads():
        copy_po.start()
        lax.fori_loop(0, 32, pieces, 0)
        copy_st.start()

    def sides(ty):
        if ty == 0:
            return wg, z, x, xm, xp, zm, zp
        return wd, x, z, zm, zp, xm, xp

    def rc(ty, k, i, ref, d):
        return pltpu.make_async_remote_copy(
            src_ref=ref, dst_ref=ref, send_sem=ssem.at[ty, i], recv_sem=rsem.at[ty, i, k],
            device_id=d, device_id_type=MESH,
        )

    def msgs(ty, k):
        buf, a, b, bm, bp, am, ap = sides(ty)
        own = buf.at[k, c]
        am1, ap1, ap2 = (a + 3) % 4, (a + 1) % 4, (a + 2) % 4
        bm1, bp1, bp2 = (b + 3) % 4, (b + 1) % 4, (b + 2) % 4
        return (
            [(0, own.at[a, b], bp, own.at[a, bm1]), (1, own.at[a, b], bm, own.at[a, bp1])],
            [
                (2, own.at[a, bm1, 0:64], bp, own.at[a, bp2, 0:64]),
                (3, own.at[a, bp1, 64:128], bm, own.at[a, bp2, 64:128]),
            ],
            [(4, own.at[a], ap, own.at[am1]), (5, own.at[a], am, own.at[ap1])],
            [(6, own.at[am1, 0:2], ap, own.at[ap2, 0:2]), (7, own.at[ap1, 2:4], am, own.at[ap2, 2:4])],
        )

    def start(ty, k, phase):
        for i, ref, d, _ in msgs(ty, k)[phase]:
            rc(ty, k, i, ref, d).start()

    def arrived(ty, k, phase):
        for i, _, d, ref in msgs(ty, k)[phase]:
            rc(ty, k, i, ref, d).wait_recv()

    def shared(ty, k, i):
        buf, a, *_ = sides(ty)
        ref = buf.at[k, c, (a + (0, 3, 1, 2)[i]) % 4]
        return pltpu.make_async_remote_copy(
            src_ref=ref, dst_ref=ref, send_sem=sibs.at[ty, i], recv_sem=sibr.at[ty, i // 3, k],
            device_id=sib, device_id_type=MESH,
        )

    def from_sibling(ty, k, last):
        ref = sides(ty)[0].at[k, 1 - c, 3:4] if last else sides(ty)[0].at[k, 1 - c, 0:3]
        return pltpu.make_async_remote_copy(
            src_ref=ref, dst_ref=ref, send_sem=sibs.at[ty, 0], recv_sem=sibr.at[ty, last, k],
            device_id=sib, device_id_type=MESH,
        )

    def within(k):
        if isinstance(k, int):
            return lambda f: f() if 0 <= k < chunks else None
        return pl.when(jnp.logical_and(k >= 0, k < chunks))

    def first_hop(j):
        @within(j + AHEAD1)
        def _():
            for ty in range(2):
                start(ty, j + AHEAD1, 0)

    def second_hop(j):
        @within(j + AHEAD2)
        def _():
            for ty in range(2):
                arrived(ty, j + AHEAD2, 0)
                start(ty, j + AHEAD2, 1)

    def third_hop(j):
        @within(j + AHEAD3)
        def _():
            for ty in range(2):
                arrived(ty, j + AHEAD3, 1)
                start(ty, j + AHEAD3, 2)
                shared(ty, j + AHEAD3, 0).start()

    def fourth_hop(j):
        @within(j)
        def _():
            for ty in range(2):
                arrived(ty, j, 2)
                start(ty, j, 3)
                shared(ty, j, 1).start()
                shared(ty, j, 2).start()

    def last_line(j):
        @within(j - 1)
        def _():
            for ty in range(2):
                arrived(ty, j - 1, 3)
                shared(ty, j - 1, 3).start()

    def product(at, ty, k, lines):
        lhs, rhs = (xv, wg) if ty == 0 else (gv, wd)
        total = None
        for line in lines:
            for cc in range(2):
                cols = pl.ds(pl.multiple_of((cc * 4 + line) * 512, 512), 512)
                term = jnp.dot(lhs[at, cols], rhs[k, cc, line].reshape(512, CHUNK), preferred_element_type=F32)
                total = term if total is None else total + term
        return total

    def most(j, part):
        @within(j)
        def _():
            at = pl.ds(part * TILE, TILE)
            for ty in range(2):
                if part == 0:
                    from_sibling(ty, j, 0).wait_recv()
            for ty in range(2):
                a = (z, x)[ty]
                acc[ty, at, :] = product(at, ty, j, [a, (a + 1) % 4, (a + 3) % 4])

    def rest(j, part):
        @within(j - 1)
        def _():
            k = j - 1
            at = pl.ds(part * TILE, TILE)
            for ty in range(2):
                if part == 0:
                    from_sibling(ty, k, 1).wait_recv()
            proj = po2[pl.ds(pl.multiple_of(k * CHUNK, CHUNK), CHUNK), :]
            gate = acc[0, at, :] + product(at, 0, k, [(z + 2) % 4])
            back = acc[1, at, :] + product(at, 1, k, [(x + 2) % 4])
            update = (back * (gate / (1.0 + jnp.exp(-gate)))).astype(BF16)
            right[at, :] += jnp.dot(update, proj, preferred_element_type=F32)

    def tables():
        row = es_ref[...]
        diag = iota((192, 192), 0) == iota((192, 192), 1)
        col = jnp.sum(jnp.where(diag, row, 0), axis=1, keepdims=True)
        same = jnp.logical_and(row == col, iota((192, 192), 0) < iota((192, 192), 1))
        rank = jnp.sum(same.astype(I32), axis=0, keepdims=True)
        rank = jnp.sum(jnp.where(diag, rank, 0), axis=1, keepdims=True)
        here = col * PAD + (rank // 6) * 8 + rank % 6
        slot[...] = here
        pos = iota((192, 256), 1)
        n, q = pos // 8, pos % 8
        ev = ((((n // 4) % 4) * 4 + n % 4) * 2 + n // 16) * 6 + q
        pick = jnp.logical_and(ev == iota((192, 256), 0), q < 6)
        target = jnp.sum(jnp.where(pick, here + 1, 0), axis=0, keepdims=True) - 1
        place[...] = (iota((256, 256), 0) == target).astype(F32).astype(BF16)

    def projections():
        right[...] = jnp.zeros_like(right)
        copy_po.wait()
        side = po[...].T
        po2[...] = jnp.concatenate([side, side], axis=1)
        pltpu.make_async_copy(x_in, xv, lsem.at[1]).wait()
        pltpu.make_async_copy(pin_in, pin, lsem.at[3]).wait()
        to = iota((64, 64), 0)
        order = (iota((64, 64), 1) == jnp.where(to < 32, 2 * to, 2 * to - 63)).astype(F32).astype(BF16)
        pin[...] = jnp.dot(order, pin[...], preferred_element_type=F32).astype(BF16)

    def lefts(m):
        lt[m] = lax.dot_general(pin[...], xv[m * SEQ : (m + 1) * SEQ, :], NT, preferred_element_type=F32)

    work = {
        0: [loads],
        1: [tables],
        2: [projections],
    }
    for m in range(seqs):
        work.setdefault(3 + m // 2, []).append(functools.partial(lefts, m))
    for j in range(AHEAD1):
        for f in (first_hop, second_hop, third_hop):
            f(j - AHEAD1)
        for f in work.get(j, []):
            f()
    pltpu.make_async_copy(g_in, gv, lsem.at[2]).wait()
    copy_st.wait()

    steps = {
        "a": first_hop, "b": second_hop, "c": third_hop, "d": fourth_hop, "e": last_line,
        "m": functools.partial(most, part=0), "M": functools.partial(most, part=1),
        "r": functools.partial(rest, part=0), "R": functools.partial(rest, part=1),
    }

    def steady(j, _):
        for name in ORDER:
            steps[name](j)
        return 0

    lax.fori_loop(0, chunks + 1, steady, 0)

    lane = iota((32, 128), 1)
    for m in range(seqs):
        both = jnp.dot(lt[m], right[m * SEQ : (m + 1) * SEQ, :], precision=HIGH, preferred_element_type=F32)
        flat = jnp.where(lane < 64, both[0:32], both[32:64])
        for u in range(4):
            pout[u, m] = flat[u * 8 : u * 8 + 8]

    def quarter(i, to, at):
        return pltpu.make_async_remote_copy(
            src_ref=pout.at[to], dst_ref=rbuf.at[at], send_sem=ysem.at[i], recv_sem=yrem.at[i],
            device_id=(s, to), device_id_type=MESH,
        )

    for i in (1, 0, 2):
        quarter(i, (t + i + 1) % 4, t).start()
    for ty in range(2):
        buf, a, b, bm, bp, am, ap = sides(ty)
        own_buf = buf.at[:, c]
        sizes = [
            own_buf.at[:, a, b], own_buf.at[:, a, b], own_buf.at[:, a, b, 0:64], own_buf.at[:, a, b, 0:64],
            own_buf.at[:, a], own_buf.at[:, a], own_buf.at[:, a, 0:2], own_buf.at[:, a, 0:2],
        ]
        for i, ref in enumerate(sizes):
            rc(ty, 0, i, ref, xm).wait_send()
        for i in range(4):
            ref = own_buf.at[:, a]
            pltpu.make_async_remote_copy(
                src_ref=ref, dst_ref=ref, send_sem=sibs.at[ty, i], recv_sem=sibr.at[ty, 0, 0],
                device_id=sib, device_id_type=MESH,
            ).wait_send()
    total = pout[t]
    for i in range(3):
        quarter(i, (t + i + 1) % 4, (t + 3 - i) % 4).wait_recv()
        total += rbuf[(t + 3 - i) % 4]
    mine = (total * (1.0 / SEQ)).reshape(seqs * 8, 128).astype(BF16)
    to, fr = iota((64, 48), 0), iota((64, 48), 1)
    turn = jnp.logical_and(fr // 8 == to % 8, fr % 8 == to // 8).astype(F32).astype(BF16)
    gat[c, z, x] = jnp.dot(turn, mine, preferred_element_type=F32).astype(BF16)

    def flat_copy(i, zz, xx):
        return pltpu.make_async_remote_copy(
            src_ref=gat.at[c, zz, xx], dst_ref=gat.at[c, zz, xx], send_sem=psem.at[i], recv_sem=prem.at[i],
            device_id=dev(z + i // 4, x + i % 4, c), device_id_type=MESH,
        )

    for i in (10, 6, 14, 9, 11, 2, 8, 5, 7, 13, 15, 1, 3, 4, 12):
        flat_copy(i, z, x).start()

    def flat_shared(ref):
        return pltpu.make_async_remote_copy(
            src_ref=ref, dst_ref=ref, send_sem=tsem, recv_sem=trem, device_id=sib, device_id_type=MESH
        )

    flat_shared(gat.at[c, z, x]).start()
    for i in (1, 3, 4, 12, 5, 7, 13, 15, 2, 8, 6, 14, 9, 11, 10):
        zz, xx = (z + 4 - i // 4) % 4, (x + 4 - i % 4) % 4
        flat_copy(i, zz, xx).wait_recv()
        flat_shared(gat.at[c, zz, xx]).start()
    flat_shared(gat.at[1 - c]).wait_recv()
    flats = gat[...].reshape(32, 64, 128).astype(F32)
    lines = [flats[:, kk * 8 : kk * 8 + 8, :].reshape(256, 128).astype(BF16) for kk in range(8)]
    placed = jnp.dot(place[...], jnp.concatenate(lines, axis=1), preferred_element_type=F32)
    grouped[...] = placed.astype(BF16).reshape(grouped.shape)

    def part_copy(g, i, to, at):
        some = pl.ds(g * 8, 8)
        return pltpu.make_async_remote_copy(
            src_ref=part.at[to, some], dst_ref=got.at[at, some], send_sem=qsem.at[g, i], recv_sem=qrem.at[g, i],
            device_id=(s, to), device_id_type=MESH,
        )

    def full_copy(g, i, to, at):
        ref = full.at[at, pl.ds(g * 8, 8)]
        return pltpu.make_async_remote_copy(
            src_ref=ref, dst_ref=ref, send_sem=fsem.at[g, i], recv_sem=frem.at[g, i],
            device_id=(s, to), device_id_type=MESH,
        )

    for g in range(2):

        first = g * 8
        found = []
        for b in range(2 * first, 2 * first + 16):
            stored = st[b * BLOCK : (b + 1) * BLOCK, :]
            found.append(lax.dot_general(grouped[bs_ref[b]], stored, NT, preferred_element_type=F32))
        for m in range(8):
            for u in range(4):
                both = [r[u * 8 : u * 8 + 8] for r in found[2 * m : 2 * m + 2]]
                part[u, first + m] = jnp.concatenate(both, axis=0).astype(BF16)
        for i in (1, 0, 2):
            part_copy(g, i, (t + i + 1) % 4, t).start()
    for i in range(3):
        quarter(i, (t + i + 1) % 4, t).wait_send()
    for i in range(1, 16):
        flat_copy(i, z, x).wait_send()
    flat_shared(gat.at[c]).wait_send()
    for g in range(2):
        for i in range(3):
            part_copy(g, i, (t + i + 1) % 4, (t + 3 - i) % 4).wait_recv()
        some = pl.ds(g * 8, 8)
        total = part[t, some].astype(F32)
        for i in range(3):
            total += got[(t + 3 - i) % 4, some].astype(F32)
        full[t, some] = total.astype(BF16)
        for i in (1, 0, 2):
            full_copy(g, i, (t + i + 1) % 4, t).start()
    for g in range(2):
        for i in range(3):
            part_copy(g, i, (t + i + 1) % 4, t).wait_send()

    own = slot[pl.ds(pl.multiple_of(t * 48, 8), 48), :]
    entry = iota((96, 64), 1)
    block_of = (entry // 8) % 2
    rest_of = jnp.concatenate([own, own], axis=0) - (entry // 16) * 8 - entry % 8
    rest_of = jnp.where(iota((96, 64), 0) // 48 == block_of, rest_of, -1)
    for g in range(2):
        for i in range(3):
            full_copy(g, i, (t + i + 1) % 4, (t + 3 - i) % 4).wait_recv()

        def expand(p, _):
            for e in range(4):
                m = g * 8 + p * 4 + e
                chosen = rest_of == jnp.where(block_of == 0, bs_ref[2 * m] * PAD, bs_ref[2 * m + 1] * PAD)
                summed = jnp.dot(
                    chosen.astype(F32).astype(BF16), full[:, m].reshape(64, 128), preferred_element_type=F32
                )
                at = pl.multiple_of(m * 2 * BLOCK, 2 * BLOCK)
                out[:, pl.ds(at, BLOCK)] = summed[0:48]
                out[:, pl.ds(at + BLOCK, BLOCK)] = summed[48:96]
            return 0

        lax.fori_loop(0, 2, expand, 0)
    for g in range(2):
        for i in range(3):
            full_copy(g, i, (t + i + 1) % 4, t).wait_send()


def local(eval_inputs, eval_grads, w_gate, w_down, proj_in, proj_out, store_rows, eval_strata, block_strata):
    tokens, width = eval_inputs.shape
    cols = w_gate.shape[1]
    chunks = cols // CHUNK
    rows, feats = store_rows.shape
    any_space = pl.BlockSpec(memory_space=pl.ANY)
    dma = pltpu.SemaphoreType.DMA
    evals = eval_strata.shape[0]
    seqs = tokens // SEQ
    return pl.pallas_call(
        kernel,
        out_shape=jax.ShapeDtypeStruct((evals // 4, rows), F32),
        in_specs=[any_space] * 7
        + [pl.BlockSpec(memory_space=pltpu.VMEM), pl.BlockSpec(memory_space=pltpu.SMEM)],
        out_specs=pl.BlockSpec(memory_space=pltpu.VMEM),
        scratch_shapes=[
            pltpu.VMEM((chunks, 2, 4, 4, 128, CHUNK), BF16),
            pltpu.VMEM((chunks, 2, 4, 4, 128, CHUNK), BF16),
            pltpu.VMEM((tokens, width), BF16),
            pltpu.VMEM((tokens, width), BF16),
            pltpu.VMEM((rows, feats), BF16),
            pltpu.VMEM((cols, 128), BF16),
            pltpu.VMEM((RANK, width), BF16),
            pltpu.VMEM((RANK, cols), BF16),
            pltpu.VMEM((cols, 2 * RANK), BF16),
            pltpu.VMEM((seqs, RANK, SEQ), F32),
            pltpu.VMEM((2, tokens, CHUNK), F32),
            pltpu.VMEM((tokens, 2 * RANK), F32),
            pltpu.VMEM((4, seqs, 8, 128), F32),
            pltpu.VMEM((4, seqs, 8, 128), F32),
            pltpu.VMEM((2, 4, 4, 64, 128), BF16),
            pltpu.VMEM((STRATA, PAD, feats), BF16),
            pltpu.VMEM((256, 256), BF16),
            pltpu.VMEM((4, rows // (2 * BLOCK), 16, BLOCK), BF16),
            pltpu.VMEM((4, rows // (2 * BLOCK), 16, BLOCK), BF16),
            pltpu.VMEM((4, rows // (2 * BLOCK), 16, BLOCK), BF16),
            pltpu.VMEM((evals, 1), I32),
            dma((6,)),
            dma((chunks,)),
            dma((2, 8)),
            dma((2, 8, chunks)),
            dma((2, 4)),
            dma((2, 2, chunks)),
            dma((3,)),
            dma((3,)),
            dma((16,)),
            dma((16,)),
            dma((2, 3)),
            dma((2, 3)),
            dma((2, 3)),
            dma((2, 3)),
            dma,
            dma,
        ],
        compiler_params=pltpu.CompilerParams(
            collective_id=0, has_side_effects=True, vmem_limit_bytes=57 * 2**20
        ),
    )(
        eval_inputs, eval_grads, w_gate, w_down, proj_in.T, proj_out.T, store_rows,
        eval_strata.reshape(1, evals), block_strata,
    )


def solution(mesh):
    return jax.shard_map(
        local,
        mesh=mesh,
        in_specs=(
            P("store", None),
            P("store", None),
            P("store", "tensor"),
            P("tensor", "store"),
            P(),
            P("tensor", None),
            P("store", "tensor"),
            P(),
            P("store"),
        ),
        out_specs=P("tensor", "store"),
        check_vma=False,
    )
```

```python
import functools

import jax
import jax.numpy as jnp
from jax import lax
from jax.experimental import pallas as pl
from jax.experimental.pallas import tpu as pltpu
from jax.sharding import PartitionSpec as P

MESH = pl.DeviceIdType.MESH
RANK, SEQ, BLOCK, STRATA = 64, 128, 128, 8
PAD = 32
CHUNK = 256
AHEAD1, AHEAD2, AHEAD3 = 8, 4, 2
ORDER = "edabcrm"
BF16, F32, I32 = jnp.bfloat16, jnp.float32, jnp.int32
HIGH = lax.Precision.HIGHEST
NT = (((1,), (1,)), ((), ()))


def iota(shape, dim):
    return lax.broadcasted_iota(I32, shape, dim)


def kernel(
    x_in, g_in, wg_in, wd_in, pin_in, po_in, st_in, es_ref, bs_ref,
    out,
    wg, wd, xv, gv, st, raw, pin, po, po2, lt, acc, right, pout, rbuf, gat, grouped, place, part, got, full, slot,
    lsem, osem, ssem, rsem, sibs, sibr, ysem, yrem, psem, prem, qsem, qrem, fsem, frem, tsem, trem,
):
    chunks, tokens = wg.shape[0], xv.shape[0]
    seqs = tokens // SEQ
    s, t = lax.axis_index("store"), lax.axis_index("tensor")
    c, x, z = s % 2, (s // 2) % 4, s // 8

    def dev(zz, xx, cc):
        return (((zz % 4) * 4 + xx % 4) * 2 + cc, t)

    xm, xp, zm, zp = dev(z, x + 3, c), dev(z, x + 1, c), dev(z + 3, x, c), dev(z + 1, x, c)
    sib = dev(z, x, 1 - c)
    ypeer = [(s, (t + i) % 4) for i in (1, 2, 3)]

    barrier = pltpu.get_barrier_semaphore()
    for d in [xm, xp, zm, zp, sib] + ypeer:
        pl.semaphore_signal(barrier, inc=1, device_id=d, device_id_type=MESH)

    copy_raw = pltpu.make_async_copy(wd_in, raw, lsem.at[0])
    copy_raw.start()

    def own_gate(k):
        return pltpu.make_async_copy(
            wg_in.at[:, pl.ds(pl.multiple_of(k * CHUNK, CHUNK), CHUNK)], wg.at[k, c, z, x], osem.at[k]
        )

    for k in range(chunks):
        own_gate(k).start()

    copy_raw.wait()
    for k in range(chunks):
        wd[k, c, x, z] = raw[k * CHUNK : (k + 1) * CHUNK, :].T
    for k in range(chunks):
        own_gate(k).wait()
    pl.semaphore_wait(barrier, 8)

    def pieces(n, _):
        cc, hi, lo = n // 16, (n // 4) % 4, n % 4
        to = pl.ds(pl.multiple_of(n * 128, 128), 128)
        a = pl.ds(pl.multiple_of(((hi * 4 + lo) * 2 + cc) * 128, 128), 128)
        b = pl.ds(pl.multiple_of(((lo * 4 + hi) * 2 + cc) * 128, 128), 128)
        pltpu.make_async_copy(x_in.at[:, a], xv.at[:, to], lsem.at[1]).start()
        pltpu.make_async_copy(g_in.at[:, b], gv.at[:, to], lsem.at[2]).start()
        pltpu.make_async_copy(pin_in.at[:, a], pin.at[:, to], lsem.at[3]).start()
        return 0

    copy_po = pltpu.make_async_copy(po_in, po, lsem.at[4])
    copy_st = pltpu.make_async_copy(st_in, st, lsem.at[5])

    def loads():
        copy_po.start()
        lax.fori_loop(0, 32, pieces, 0)
        copy_st.start()

    def sides(ty):
        if ty == 0:
            return wg, z, x, xm, xp, zm, zp
        return wd, x, z, zm, zp, xm, xp

    def rc(ty, k, i, ref, d):
        return pltpu.make_async_remote_copy(
            src_ref=ref, dst_ref=ref, send_sem=ssem.at[ty, i], recv_sem=rsem.at[ty, i, k],
            device_id=d, device_id_type=MESH,
        )

    def msgs(ty, k):
        buf, a, b, bm, bp, am, ap = sides(ty)
        own = buf.at[k, c]
        am1, ap1, ap2 = (a + 3) % 4, (a + 1) % 4, (a + 2) % 4
        bm1, bp1, bp2 = (b + 3) % 4, (b + 1) % 4, (b + 2) % 4
        return (
            [(0, own.at[a, b], bp, own.at[a, bm1]), (1, own.at[a, b], bm, own.at[a, bp1])],
            [
                (2, own.at[a, bm1, 0:64], bp, own.at[a, bp2, 0:64]),
                (3, own.at[a, bp1, 64:128], bm, own.at[a, bp2, 64:128]),
            ],
            [(4, own.at[a], ap, own.at[am1]), (5, own.at[a], am, own.at[ap1])],
            [(6, own.at[am1, 0:2], ap, own.at[ap2, 0:2]), (7, own.at[ap1, 2:4], am, own.at[ap2, 2:4])],
        )

    def start(ty, k, phase):
        for i, ref, d, _ in msgs(ty, k)[phase]:
            rc(ty, k, i, ref, d).start()

    def arrived(ty, k, phase):
        for i, _, d, ref in msgs(ty, k)[phase]:
            rc(ty, k, i, ref, d).wait_recv()

    def shared(ty, k, i):
        buf, a, *_ = sides(ty)
        ref = buf.at[k, c, (a + (0, 3, 1, 2)[i]) % 4]
        return pltpu.make_async_remote_copy(
            src_ref=ref, dst_ref=ref, send_sem=sibs.at[ty, i], recv_sem=sibr.at[ty, i // 3, k],
            device_id=sib, device_id_type=MESH,
        )

    def from_sibling(ty, k, last):
        ref = sides(ty)[0].at[k, 1 - c, 3:4] if last else sides(ty)[0].at[k, 1 - c, 0:3]
        return pltpu.make_async_remote_copy(
            src_ref=ref, dst_ref=ref, send_sem=sibs.at[ty, 0], recv_sem=sibr.at[ty, last, k],
            device_id=sib, device_id_type=MESH,
        )

    def within(k):
        if isinstance(k, int):
            return lambda f: f() if 0 <= k < chunks else None
        return pl.when(jnp.logical_and(k >= 0, k < chunks))

    def first_hop(j):
        @within(j + AHEAD1)
        def _():
            for ty in range(2):
                start(ty, j + AHEAD1, 0)

    def second_hop(j):
        @within(j + AHEAD2)
        def _():
            for ty in range(2):
                arrived(ty, j + AHEAD2, 0)
                start(ty, j + AHEAD2, 1)

    def third_hop(j):
        @within(j + AHEAD3)
        def _():
            for ty in range(2):
                arrived(ty, j + AHEAD3, 1)
                start(ty, j + AHEAD3, 2)
                shared(ty, j + AHEAD3, 0).start()

    def fourth_hop(j):
        @within(j)
        def _():
            for ty in range(2):
                arrived(ty, j, 2)
                start(ty, j, 3)
                shared(ty, j, 1).start()
                shared(ty, j, 2).start()

    def last_line(j):
        @within(j - 1)
        def _():
            for ty in range(2):
                arrived(ty, j - 1, 3)
                shared(ty, j - 1, 3).start()

    def product(at, ty, k, lines):
        lhs, rhs = (xv, wg) if ty == 0 else (gv, wd)
        total = None
        for line in lines:
            for cc in range(2):
                cols = pl.ds(pl.multiple_of((cc * 4 + line) * 512, 512), 512)
                term = jnp.dot(lhs[at, cols], rhs[k, cc, line].reshape(512, CHUNK), preferred_element_type=F32)
                total = term if total is None else total + term
        return total

    def most(j):
        @within(j)
        def _():
            at = slice(None)
            for ty in range(2):
                from_sibling(ty, j, 0).wait_recv()
            for ty in range(2):
                a = (z, x)[ty]
                acc[ty, at, :] = product(at, ty, j, [a, (a + 1) % 4, (a + 3) % 4])

    def rest(j):
        @within(j - 1)
        def _():
            k = j - 1
            at = slice(None)
            for ty in range(2):
                from_sibling(ty, k, 1).wait_recv()
            proj = po2[pl.ds(pl.multiple_of(k * CHUNK, CHUNK), CHUNK), :]
            gate = acc[0, at, :] + product(at, 0, k, [(z + 2) % 4])
            back = acc[1, at, :] + product(at, 1, k, [(x + 2) % 4])
            update = (back * (gate / (1.0 + jnp.exp(-gate)))).astype(BF16)
            right[at, :] += jnp.dot(update, proj, preferred_element_type=F32)

    def tables():
        row = es_ref[...]
        diag = iota((192, 192), 0) == iota((192, 192), 1)
        col = jnp.sum(jnp.where(diag, row, 0), axis=1, keepdims=True)
        same = jnp.logical_and(row == col, iota((192, 192), 0) < iota((192, 192), 1))
        rank = jnp.sum(same.astype(I32), axis=0, keepdims=True)
        rank = jnp.sum(jnp.where(diag, rank, 0), axis=1, keepdims=True)
        here = col * PAD + (rank // 6) * 8 + rank % 6
        slot[...] = here
        pos = iota((192, 256), 1)
        n, q = pos // 8, pos % 8
        ev = ((((n // 4) % 4) * 4 + n % 4) * 2 + n // 16) * 6 + q
        pick = jnp.logical_and(ev == iota((192, 256), 0), q < 6)
        target = jnp.sum(jnp.where(pick, here + 1, 0), axis=0, keepdims=True) - 1
        place[...] = (iota((256, 256), 0) == target).astype(F32).astype(BF16)

    def projections():
        right[...] = jnp.zeros_like(right)
        copy_po.wait()
        side = po[...].T
        po2[...] = jnp.concatenate([side, side], axis=1)
        pltpu.make_async_copy(x_in, xv, lsem.at[1]).wait()
        pltpu.make_async_copy(pin_in, pin, lsem.at[3]).wait()
        to = iota((64, 64), 0)
        order = (iota((64, 64), 1) == jnp.where(to < 32, 2 * to, 2 * to - 63)).astype(F32).astype(BF16)
        pin[...] = jnp.dot(order, pin[...], preferred_element_type=F32).astype(BF16)

    def lefts(m):
        lt[m] = lax.dot_general(pin[...], xv[m * SEQ : (m + 1) * SEQ, :], NT, preferred_element_type=F32)

    work = {
        2: [loads],
        3: [tables],
        4: [projections],
    }
    for m in range(seqs):
        work.setdefault(5 + m // 2, []).append(functools.partial(lefts, m))
    for j in range(AHEAD1):
        for f in (first_hop, second_hop, third_hop):
            f(j - AHEAD1)
        for f in work.get(j, []):
            f()
    pltpu.make_async_copy(g_in, gv, lsem.at[2]).wait()
    copy_st.wait()

    steps = {
        "a": first_hop, "b": second_hop, "c": third_hop, "d": fourth_hop, "e": last_line,
        "m": most, "r": rest,
    }

    def steady(j, _):
        for name in ORDER:
            steps[name](j)
        return 0

    lax.fori_loop(0, chunks + 1, steady, 0)

    lane = iota((32, 128), 1)
    for m in range(seqs):
        both = jnp.dot(lt[m], right[m * SEQ : (m + 1) * SEQ, :], precision=HIGH, preferred_element_type=F32)
        flat = jnp.where(lane < 64, both[0:32], both[32:64])
        for u in range(4):
            pout[u, m] = flat[u * 8 : u * 8 + 8]

    def quarter(i, to, at):
        return pltpu.make_async_remote_copy(
            src_ref=pout.at[to], dst_ref=rbuf.at[at], send_sem=ysem.at[i], recv_sem=yrem.at[i],
            device_id=(s, to), device_id_type=MESH,
        )

    for i in (1, 0, 2):
        quarter(i, (t + i + 1) % 4, t).start()
    for ty in range(2):
        buf, a, b, bm, bp, am, ap = sides(ty)
        own_buf = buf.at[:, c]
        sizes = [
            own_buf.at[:, a, b], own_buf.at[:, a, b], own_buf.at[:, a, b, 0:64], own_buf.at[:, a, b, 0:64],
            own_buf.at[:, a], own_buf.at[:, a], own_buf.at[:, a, 0:2], own_buf.at[:, a, 0:2],
        ]
        for i, ref in enumerate(sizes):
            rc(ty, 0, i, ref, xm).wait_send()
        for i in range(4):
            ref = own_buf.at[:, a]
            pltpu.make_async_remote_copy(
                src_ref=ref, dst_ref=ref, send_sem=sibs.at[ty, i], recv_sem=sibr.at[ty, 0, 0],
                device_id=sib, device_id_type=MESH,
            ).wait_send()
    total = pout[t]
    for i in range(3):
        quarter(i, (t + i + 1) % 4, (t + 3 - i) % 4).wait_recv()
        total += rbuf[(t + 3 - i) % 4]
    mine = (total * (1.0 / SEQ)).reshape(seqs * 8, 128).astype(BF16)
    to, fr = iota((64, 48), 0), iota((64, 48), 1)
    turn = jnp.logical_and(fr // 8 == to % 8, fr % 8 == to // 8).astype(F32).astype(BF16)
    gat[c, z, x] = jnp.dot(turn, mine, preferred_element_type=F32).astype(BF16)

    def flat_copy(i, zz, xx):
        return pltpu.make_async_remote_copy(
            src_ref=gat.at[c, zz, xx], dst_ref=gat.at[c, zz, xx], send_sem=psem.at[i], recv_sem=prem.at[i],
            device_id=dev(z + i // 4, x + i % 4, c), device_id_type=MESH,
        )

    for i in (10, 6, 14, 9, 11, 2, 8, 5, 7, 13, 15, 1, 3, 4, 12):
        flat_copy(i, z, x).start()

    def flat_shared(ref):
        return pltpu.make_async_remote_copy(
            src_ref=ref, dst_ref=ref, send_sem=tsem, recv_sem=trem, device_id=sib, device_id_type=MESH
        )

    flat_shared(gat.at[c, z, x]).start()
    for i in (1, 3, 4, 12, 5, 7, 13, 15, 2, 8, 6, 14, 9, 11, 10):
        zz, xx = (z + 4 - i // 4) % 4, (x + 4 - i % 4) % 4
        flat_copy(i, zz, xx).wait_recv()
        flat_shared(gat.at[c, zz, xx]).start()
    flat_shared(gat.at[1 - c]).wait_recv()
    flats = gat[...].reshape(32, 64, 128).astype(F32)
    lines = [flats[:, kk * 8 : kk * 8 + 8, :].reshape(256, 128).astype(BF16) for kk in range(8)]
    placed = jnp.dot(place[...], jnp.concatenate(lines, axis=1), preferred_element_type=F32)
    grouped[...] = placed.astype(BF16).reshape(grouped.shape)

    def part_copy(g, i, to, at):
        some = pl.ds(g * 8, 8)
        return pltpu.make_async_remote_copy(
            src_ref=part.at[to, some], dst_ref=got.at[at, some], send_sem=qsem.at[g, i], recv_sem=qrem.at[g, i],
            device_id=(s, to), device_id_type=MESH,
        )

    def full_copy(g, i, to, at):
        ref = full.at[at, pl.ds(g * 8, 8)]
        return pltpu.make_async_remote_copy(
            src_ref=ref, dst_ref=ref, send_sem=fsem.at[g, i], recv_sem=frem.at[g, i],
            device_id=(s, to), device_id_type=MESH,
        )

    for g in range(2):

        first = g * 8
        found = []
        for b in range(2 * first, 2 * first + 16):
            stored = st[b * BLOCK : (b + 1) * BLOCK, :]
            found.append(lax.dot_general(grouped[bs_ref[b]], stored, NT, preferred_element_type=F32))
        for m in range(8):
            for u in range(4):
                both = [r[u * 8 : u * 8 + 8] for r in found[2 * m : 2 * m + 2]]
                part[u, first + m] = jnp.concatenate(both, axis=0).astype(BF16)
        for i in (1, 0, 2):
            part_copy(g, i, (t + i + 1) % 4, t).start()
    for i in range(3):
        quarter(i, (t + i + 1) % 4, t).wait_send()
    for i in range(1, 16):
        flat_copy(i, z, x).wait_send()
    flat_shared(gat.at[c]).wait_send()
    for g in range(2):
        for i in range(3):
            part_copy(g, i, (t + i + 1) % 4, (t + 3 - i) % 4).wait_recv()
        some = pl.ds(g * 8, 8)
        total = part[t, some].astype(F32)
        for i in range(3):
            total += got[(t + 3 - i) % 4, some].astype(F32)
        full[t, some] = total.astype(BF16)
        for i in (1, 0, 2):
            full_copy(g, i, (t + i + 1) % 4, t).start()
    for g in range(2):
        for i in range(3):
            part_copy(g, i, (t + i + 1) % 4, t).wait_send()

    own = slot[pl.ds(pl.multiple_of(t * 48, 8), 48), :]
    entry = iota((96, 64), 1)
    block_of = (entry // 8) % 2
    rest_of = jnp.concatenate([own, own], axis=0) - (entry // 16) * 8 - entry % 8
    rest_of = jnp.where(iota((96, 64), 0) // 48 == block_of, rest_of, -1)
    for g in range(2):
        for i in range(3):
            full_copy(g, i, (t + i + 1) % 4, (t + 3 - i) % 4).wait_recv()

        def expand(p, _):
            for e in range(4):
                m = g * 8 + p * 4 + e
                chosen = rest_of == jnp.where(block_of == 0, bs_ref[2 * m] * PAD, bs_ref[2 * m + 1] * PAD)
                summed = jnp.dot(
                    chosen.astype(F32).astype(BF16), full[:, m].reshape(64, 128), preferred_element_type=F32
                )
                at = pl.multiple_of(m * 2 * BLOCK, 2 * BLOCK)
                out[:, pl.ds(at, BLOCK)] = summed[0:48]
                out[:, pl.ds(at + BLOCK, BLOCK)] = summed[48:96]
            return 0

        lax.fori_loop(0, 2, expand, 0)
    for g in range(2):
        for i in range(3):
            full_copy(g, i, (t + i + 1) % 4, t).wait_send()


def local(eval_inputs, eval_grads, w_gate, w_down, proj_in, proj_out, store_rows, eval_strata, block_strata):
    tokens, width = eval_inputs.shape
    cols = w_gate.shape[1]
    chunks = cols // CHUNK
    rows, feats = store_rows.shape
    any_space = pl.BlockSpec(memory_space=pl.ANY)
    dma = pltpu.SemaphoreType.DMA
    evals = eval_strata.shape[0]
    seqs = tokens // SEQ
    return pl.pallas_call(
        kernel,
        out_shape=jax.ShapeDtypeStruct((evals // 4, rows), F32),
        in_specs=[any_space] * 7
        + [pl.BlockSpec(memory_space=pltpu.VMEM), pl.BlockSpec(memory_space=pltpu.SMEM)],
        out_specs=pl.BlockSpec(memory_space=pltpu.VMEM),
        scratch_shapes=[
            pltpu.VMEM((chunks, 2, 4, 4, 128, CHUNK), BF16),
            pltpu.VMEM((chunks, 2, 4, 4, 128, CHUNK), BF16),
            pltpu.VMEM((tokens, width), BF16),
            pltpu.VMEM((tokens, width), BF16),
            pltpu.VMEM((rows, feats), BF16),
            pltpu.VMEM((cols, 128), BF16),
            pltpu.VMEM((RANK, width), BF16),
            pltpu.VMEM((RANK, cols), BF16),
            pltpu.VMEM((cols, 2 * RANK), BF16),
            pltpu.VMEM((seqs, RANK, SEQ), F32),
            pltpu.VMEM((2, tokens, CHUNK), F32),
            pltpu.VMEM((tokens, 2 * RANK), F32),
            pltpu.VMEM((4, seqs, 8, 128), F32),
            pltpu.VMEM((4, seqs, 8, 128), F32),
            pltpu.VMEM((2, 4, 4, 64, 128), BF16),
            pltpu.VMEM((STRATA, PAD, feats), BF16),
            pltpu.VMEM((256, 256), BF16),
            pltpu.VMEM((4, rows // (2 * BLOCK), 16, BLOCK), BF16),
            pltpu.VMEM((4, rows // (2 * BLOCK), 16, BLOCK), BF16),
            pltpu.VMEM((4, rows // (2 * BLOCK), 16, BLOCK), BF16),
            pltpu.VMEM((evals, 1), I32),
            dma((6,)),
            dma((chunks,)),
            dma((2, 8)),
            dma((2, 8, chunks)),
            dma((2, 4)),
            dma((2, 2, chunks)),
            dma((3,)),
            dma((3,)),
            dma((16,)),
            dma((16,)),
            dma((2, 3)),
            dma((2, 3)),
            dma((2, 3)),
            dma((2, 3)),
            dma,
            dma,
        ],
        compiler_params=pltpu.CompilerParams(
            collective_id=0, has_side_effects=True, vmem_limit_bytes=57 * 2**20
        ),
    )(
        eval_inputs, eval_grads, w_gate, w_down, proj_in.T, proj_out.T, store_rows,
        eval_strata.reshape(1, evals), block_strata,
    )


def solution(mesh):
    return jax.shard_map(
        local,
        mesh=mesh,
        in_specs=(
            P("store", None),
            P("store", None),
            P("store", "tensor"),
            P("tensor", "store"),
            P(),
            P("tensor", None),
            P("store", "tensor"),
            P(),
            P("store"),
        ),
        out_specs=P("tensor", "store"),
        check_vma=False,
    )
```

```python
import functools

import jax
import jax.numpy as jnp
from jax import lax
from jax.experimental import pallas as pl
from jax.experimental.pallas import tpu as pltpu
from jax.sharding import PartitionSpec as P

MESH = pl.DeviceIdType.MESH
RANK, SEQ, BLOCK, STRATA = 64, 128, 128, 8
PAD = 32
CHUNK = 256
AHEAD1, AHEAD2, AHEAD3 = 8, 4, 2
ORDER = "derabcm"
BF16, F32, I32 = jnp.bfloat16, jnp.float32, jnp.int32
HIGH = lax.Precision.HIGHEST
NT = (((1,), (1,)), ((), ()))


def iota(shape, dim):
    return lax.broadcasted_iota(I32, shape, dim)


def kernel(
    x_in, g_in, wg_in, wd_in, pin_in, po_in, st_in, es_ref, bs_ref,
    out,
    wg, wd, xv, gv, st, raw, pin, po, po2, lt, acc, right, pout, rbuf, gat, grouped, place, part, got, full, slot,
    lsem, osem, ssem, rsem, sibs, sibr, ysem, yrem, psem, prem, qsem, qrem, fsem, frem, tsem, trem,
):
    chunks, tokens = wg.shape[0], xv.shape[0]
    seqs = tokens // SEQ
    s, t = lax.axis_index("store"), lax.axis_index("tensor")
    c, x, z = s % 2, (s // 2) % 4, s // 8

    def dev(zz, xx, cc):
        return (((zz % 4) * 4 + xx % 4) * 2 + cc, t)

    xm, xp, zm, zp = dev(z, x + 3, c), dev(z, x + 1, c), dev(z + 3, x, c), dev(z + 1, x, c)
    sib = dev(z, x, 1 - c)
    ypeer = [(s, (t + i) % 4) for i in (1, 2, 3)]

    barrier = pltpu.get_barrier_semaphore()
    for d in [xm, xp, zm, zp, sib] + ypeer:
        pl.semaphore_signal(barrier, inc=1, device_id=d, device_id_type=MESH)

    copy_raw = pltpu.make_async_copy(wd_in, raw, lsem.at[0])
    copy_raw.start()

    def own_gate(k):
        return pltpu.make_async_copy(
            wg_in.at[:, pl.ds(pl.multiple_of(k * CHUNK, CHUNK), CHUNK)], wg.at[k, c, z, x], osem.at[k]
        )

    for k in range(chunks):
        own_gate(k).start()

    copy_raw.wait()
    for k in range(chunks):
        wd[k, c, x, z] = raw[k * CHUNK : (k + 1) * CHUNK, :].T
    for k in range(chunks):
        own_gate(k).wait()
    pl.semaphore_wait(barrier, 8)

    def pieces(n, _):
        cc, hi, lo = n // 16, (n // 4) % 4, n % 4
        to = pl.ds(pl.multiple_of(n * 128, 128), 128)
        a = pl.ds(pl.multiple_of(((hi * 4 + lo) * 2 + cc) * 128, 128), 128)
        b = pl.ds(pl.multiple_of(((lo * 4 + hi) * 2 + cc) * 128, 128), 128)
        pltpu.make_async_copy(x_in.at[:, a], xv.at[:, to], lsem.at[1]).start()
        pltpu.make_async_copy(g_in.at[:, b], gv.at[:, to], lsem.at[2]).start()
        pltpu.make_async_copy(pin_in.at[:, a], pin.at[:, to], lsem.at[3]).start()
        return 0

    copy_po = pltpu.make_async_copy(po_in, po, lsem.at[4])
    copy_st = pltpu.make_async_copy(st_in, st, lsem.at[5])

    def loads():
        copy_po.start()
        lax.fori_loop(0, 32, pieces, 0)
        copy_st.start()

    def sides(ty):
        if ty == 0:
            return wg, z, x, xm, xp, zm, zp
        return wd, x, z, zm, zp, xm, xp

    def rc(ty, k, i, ref, d):
        return pltpu.make_async_remote_copy(
            src_ref=ref, dst_ref=ref, send_sem=ssem.at[ty, i], recv_sem=rsem.at[ty, i, k],
            device_id=d, device_id_type=MESH,
        )

    def msgs(ty, k):
        buf, a, b, bm, bp, am, ap = sides(ty)
        own = buf.at[k, c]
        am1, ap1, ap2 = (a + 3) % 4, (a + 1) % 4, (a + 2) % 4
        bm1, bp1, bp2 = (b + 3) % 4, (b + 1) % 4, (b + 2) % 4
        return (
            [(0, own.at[a, b], bp, own.at[a, bm1]), (1, own.at[a, b], bm, own.at[a, bp1])],
            [
                (2, own.at[a, bm1, 0:64], bp, own.at[a, bp2, 0:64]),
                (3, own.at[a, bp1, 64:128], bm, own.at[a, bp2, 64:128]),
            ],
            [(4, own.at[a], ap, own.at[am1]), (5, own.at[a], am, own.at[ap1])],
            [(6, own.at[am1, 0:2], ap, own.at[ap2, 0:2]), (7, own.at[ap1, 2:4], am, own.at[ap2, 2:4])],
        )

    def start(ty, k, phase):
        for i, ref, d, _ in msgs(ty, k)[phase]:
            rc(ty, k, i, ref, d).start()

    def arrived(ty, k, phase):
        for i, _, d, ref in msgs(ty, k)[phase]:
            rc(ty, k, i, ref, d).wait_recv()

    def shared(ty, k, i):
        buf, a, *_ = sides(ty)
        ref = buf.at[k, c, (a + (0, 3, 1, 2)[i]) % 4]
        return pltpu.make_async_remote_copy(
            src_ref=ref, dst_ref=ref, send_sem=sibs.at[ty, i], recv_sem=sibr.at[ty, i // 3, k],
            device_id=sib, device_id_type=MESH,
        )

    def from_sibling(ty, k, last):
        ref = sides(ty)[0].at[k, 1 - c, 3:4] if last else sides(ty)[0].at[k, 1 - c, 0:3]
        return pltpu.make_async_remote_copy(
            src_ref=ref, dst_ref=ref, send_sem=sibs.at[ty, 0], recv_sem=sibr.at[ty, last, k],
            device_id=sib, device_id_type=MESH,
        )

    def within(k):
        if isinstance(k, int):
            return lambda f: f() if 0 <= k < chunks else None
        return pl.when(jnp.logical_and(k >= 0, k < chunks))

    def first_hop(j):
        @within(j + AHEAD1)
        def _():
            for ty in range(2):
                start(ty, j + AHEAD1, 0)

    def second_hop(j):
        @within(j + AHEAD2)
        def _():
            for ty in range(2):
                arrived(ty, j + AHEAD2, 0)
                start(ty, j + AHEAD2, 1)

    def third_hop(j):
        @within(j + AHEAD3)
        def _():
            for ty in range(2):
                arrived(ty, j + AHEAD3, 1)
                start(ty, j + AHEAD3, 2)
                shared(ty, j + AHEAD3, 0).start()

    def fourth_hop(j):
        @within(j)
        def _():
            for ty in range(2):
                arrived(ty, j, 2)
                start(ty, j, 3)
                shared(ty, j, 1).start()
                shared(ty, j, 2).start()

    def last_line(j):
        @within(j - 1)
        def _():
            for ty in range(2):
                arrived(ty, j - 1, 3)
                shared(ty, j - 1, 3).start()

    def product(at, ty, k, lines):
        lhs, rhs = (xv, wg) if ty == 0 else (gv, wd)
        total = None
        for line in lines:
            for cc in range(2):
                cols = pl.ds(pl.multiple_of((cc * 4 + line) * 512, 512), 512)
                term = jnp.dot(lhs[at, cols], rhs[k, cc, line].reshape(512, CHUNK), preferred_element_type=F32)
                total = term if total is None else total + term
        return total

    def most(j):
        @within(j)
        def _():
            at = slice(None)
            for ty in range(2):
                from_sibling(ty, j, 0).wait_recv()
            for ty in range(2):
                a = (z, x)[ty]
                acc[ty, at, :] = product(at, ty, j, [a, (a + 1) % 4, (a + 3) % 4])

    def rest(j):
        @within(j - 1)
        def _():
            k = j - 1
            at = slice(None)
            for ty in range(2):
                from_sibling(ty, k, 1).wait_recv()
            proj = po2[pl.ds(pl.multiple_of(k * CHUNK, CHUNK), CHUNK), :]
            gate = acc[0, at, :] + product(at, 0, k, [(z + 2) % 4])
            back = acc[1, at, :] + product(at, 1, k, [(x + 2) % 4])
            update = (back * (gate / (1.0 + jnp.exp(-gate)))).astype(BF16)
            right[at, :] += jnp.dot(update, proj, preferred_element_type=F32)

    def tables():
        row = es_ref[...]
        diag = iota((192, 192), 0) == iota((192, 192), 1)
        col = jnp.sum(jnp.where(diag, row, 0), axis=1, keepdims=True)
        same = jnp.logical_and(row == col, iota((192, 192), 0) < iota((192, 192), 1))
        rank = jnp.sum(same.astype(I32), axis=0, keepdims=True)
        rank = jnp.sum(jnp.where(diag, rank, 0), axis=1, keepdims=True)
        here = col * PAD + (rank // 6) * 8 + rank % 6
        slot[...] = here
        pos = iota((192, 256), 1)
        n, q = pos // 8, pos % 8
        ev = ((((n // 4) % 4) * 4 + n % 4) * 2 + n // 16) * 6 + q
        pick = jnp.logical_and(ev == iota((192, 256), 0), q < 6)
        target = jnp.sum(jnp.where(pick, here + 1, 0), axis=0, keepdims=True) - 1
        place[...] = (iota((256, 256), 0) == target).astype(F32).astype(BF16)

    def projections():
        right[...] = jnp.zeros_like(right)
        copy_po.wait()
        side = po[...].T
        po2[...] = jnp.concatenate([side, side], axis=1)
        pltpu.make_async_copy(x_in, xv, lsem.at[1]).wait()
        pltpu.make_async_copy(pin_in, pin, lsem.at[3]).wait()
        to = iota((64, 64), 0)
        order = (iota((64, 64), 1) == jnp.where(to < 32, 2 * to, 2 * to - 63)).astype(F32).astype(BF16)
        pin[...] = jnp.dot(order, pin[...], preferred_element_type=F32).astype(BF16)

    def lefts(m):
        lt[m] = lax.dot_general(pin[...], xv[m * SEQ : (m + 1) * SEQ, :], NT, preferred_element_type=F32)

    work = {
        2: [loads],
        3: [tables],
        4: [projections],
    }
    for m in range(seqs):
        work.setdefault(5 + m // 2, []).append(functools.partial(lefts, m))
    for j in range(AHEAD1):
        for f in (first_hop, second_hop, third_hop):
            f(j - AHEAD1)
        for f in work.get(j, []):
            f()
    pltpu.make_async_copy(g_in, gv, lsem.at[2]).wait()
    copy_st.wait()

    steps = {
        "a": first_hop, "b": second_hop, "c": third_hop, "d": fourth_hop, "e": last_line,
        "m": most, "r": rest,
    }

    def steady(j, _):
        for name in ORDER:
            steps[name](j)
        return 0

    lax.fori_loop(0, chunks + 1, steady, 0)

    lane = iota((32, 128), 1)
    for m in range(seqs):
        both = jnp.dot(lt[m], right[m * SEQ : (m + 1) * SEQ, :], precision=HIGH, preferred_element_type=F32)
        flat = jnp.where(lane < 64, both[0:32], both[32:64])
        for u in range(4):
            pout[u, m] = flat[u * 8 : u * 8 + 8]

    def quarter(i, to, at):
        return pltpu.make_async_remote_copy(
            src_ref=pout.at[to], dst_ref=rbuf.at[at], send_sem=ysem.at[i], recv_sem=yrem.at[i],
            device_id=(s, to), device_id_type=MESH,
        )

    for i in (1, 0, 2):
        quarter(i, (t + i + 1) % 4, t).start()
    for ty in range(2):
        buf, a, b, bm, bp, am, ap = sides(ty)
        own_buf = buf.at[:, c]
        sizes = [
            own_buf.at[:, a, b], own_buf.at[:, a, b], own_buf.at[:, a, b, 0:64], own_buf.at[:, a, b, 0:64],
            own_buf.at[:, a], own_buf.at[:, a], own_buf.at[:, a, 0:2], own_buf.at[:, a, 0:2],
        ]
        for i, ref in enumerate(sizes):
            rc(ty, 0, i, ref, xm).wait_send()
        for i in range(4):
            ref = own_buf.at[:, a]
            pltpu.make_async_remote_copy(
                src_ref=ref, dst_ref=ref, send_sem=sibs.at[ty, i], recv_sem=sibr.at[ty, 0, 0],
                device_id=sib, device_id_type=MESH,
            ).wait_send()
    total = pout[t]
    for i in range(3):
        quarter(i, (t + i + 1) % 4, (t + 3 - i) % 4).wait_recv()
        total += rbuf[(t + 3 - i) % 4]
    mine = (total * (1.0 / SEQ)).reshape(seqs * 8, 128).astype(BF16)
    to, fr = iota((64, 48), 0), iota((64, 48), 1)
    turn = jnp.logical_and(fr // 8 == to % 8, fr % 8 == to // 8).astype(F32).astype(BF16)
    gat[c, z, x] = jnp.dot(turn, mine, preferred_element_type=F32).astype(BF16)

    def flat_copy(i, zz, xx):
        return pltpu.make_async_remote_copy(
            src_ref=gat.at[c, zz, xx], dst_ref=gat.at[c, zz, xx], send_sem=psem.at[i], recv_sem=prem.at[i],
            device_id=dev(z + i // 4, x + i % 4, c), device_id_type=MESH,
        )

    for i in (10, 6, 14, 9, 11, 2, 8, 5, 7, 13, 15, 1, 3, 4, 12):
        flat_copy(i, z, x).start()

    def flat_shared(ref):
        return pltpu.make_async_remote_copy(
            src_ref=ref, dst_ref=ref, send_sem=tsem, recv_sem=trem, device_id=sib, device_id_type=MESH
        )

    flat_shared(gat.at[c, z, x]).start()
    for i in (1, 3, 4, 12, 5, 7, 13, 15, 2, 8, 6, 14, 9, 11, 10):
        zz, xx = (z + 4 - i // 4) % 4, (x + 4 - i % 4) % 4
        flat_copy(i, zz, xx).wait_recv()
        flat_shared(gat.at[c, zz, xx]).start()
    flat_shared(gat.at[1 - c]).wait_recv()
    flats = gat[...].reshape(32, 64, 128).astype(F32)
    lines = [flats[:, kk * 8 : kk * 8 + 8, :].reshape(256, 128).astype(BF16) for kk in range(8)]
    placed = jnp.dot(place[...], jnp.concatenate(lines, axis=1), preferred_element_type=F32)
    grouped[...] = placed.astype(BF16).reshape(grouped.shape)

    def part_copy(g, i, to, at):
        some = pl.ds(g * 8, 8)
        return pltpu.make_async_remote_copy(
            src_ref=part.at[to, some], dst_ref=got.at[at, some], send_sem=qsem.at[g, i], recv_sem=qrem.at[g, i],
            device_id=(s, to), device_id_type=MESH,
        )

    def full_copy(g, i, to, at):
        ref = full.at[at, pl.ds(g * 8, 8)]
        return pltpu.make_async_remote_copy(
            src_ref=ref, dst_ref=ref, send_sem=fsem.at[g, i], recv_sem=frem.at[g, i],
            device_id=(s, to), device_id_type=MESH,
        )

    for g in range(2):

        first = g * 8
        found = []
        for b in range(2 * first, 2 * first + 16):
            stored = st[b * BLOCK : (b + 1) * BLOCK, :]
            found.append(lax.dot_general(grouped[bs_ref[b]], stored, NT, preferred_element_type=F32))
        for m in range(8):
            for u in range(4):
                both = [r[u * 8 : u * 8 + 8] for r in found[2 * m : 2 * m + 2]]
                part[u, first + m] = jnp.concatenate(both, axis=0).astype(BF16)
        for i in (1, 0, 2):
            part_copy(g, i, (t + i + 1) % 4, t).start()
    for i in range(3):
        quarter(i, (t + i + 1) % 4, t).wait_send()
    for i in range(1, 16):
        flat_copy(i, z, x).wait_send()
    flat_shared(gat.at[c]).wait_send()
    for g in range(2):
        for i in range(3):
            part_copy(g, i, (t + i + 1) % 4, (t + 3 - i) % 4).wait_recv()
        some = pl.ds(g * 8, 8)
        total = part[t, some].astype(F32)
        for i in range(3):
            total += got[(t + 3 - i) % 4, some].astype(F32)
        full[t, some] = total.astype(BF16)
        for i in (1, 0, 2):
            full_copy(g, i, (t + i + 1) % 4, t).start()
    for g in range(2):
        for i in range(3):
            part_copy(g, i, (t + i + 1) % 4, t).wait_send()

    own = slot[pl.ds(pl.multiple_of(t * 48, 8), 48), :]
    entry = iota((96, 64), 1)
    block_of = (entry // 8) % 2
    rest_of = jnp.concatenate([own, own], axis=0) - (entry // 16) * 8 - entry % 8
    rest_of = jnp.where(iota((96, 64), 0) // 48 == block_of, rest_of, -1)
    for g in range(2):
        for i in range(3):
            full_copy(g, i, (t + i + 1) % 4, (t + 3 - i) % 4).wait_recv()

        def expand(p, _):
            for e in range(4):
                m = g * 8 + p * 4 + e
                chosen = rest_of == jnp.where(block_of == 0, bs_ref[2 * m] * PAD, bs_ref[2 * m + 1] * PAD)
                summed = jnp.dot(
                    chosen.astype(F32).astype(BF16), full[:, m].reshape(64, 128), preferred_element_type=F32
                )
                at = pl.multiple_of(m * 2 * BLOCK, 2 * BLOCK)
                out[:, pl.ds(at, BLOCK)] = summed[0:48]
                out[:, pl.ds(at + BLOCK, BLOCK)] = summed[48:96]
            return 0

        lax.fori_loop(0, 2, expand, 0)
    for g in range(2):
        for i in range(3):
            full_copy(g, i, (t + i + 1) % 4, t).wait_send()


def local(eval_inputs, eval_grads, w_gate, w_down, proj_in, proj_out, store_rows, eval_strata, block_strata):
    tokens, width = eval_inputs.shape
    cols = w_gate.shape[1]
    chunks = cols // CHUNK
    rows, feats = store_rows.shape
    any_space = pl.BlockSpec(memory_space=pl.ANY)
    dma = pltpu.SemaphoreType.DMA
    evals = eval_strata.shape[0]
    seqs = tokens // SEQ
    return pl.pallas_call(
        kernel,
        out_shape=jax.ShapeDtypeStruct((evals // 4, rows), F32),
        in_specs=[any_space] * 7
        + [pl.BlockSpec(memory_space=pltpu.VMEM), pl.BlockSpec(memory_space=pltpu.SMEM)],
        out_specs=pl.BlockSpec(memory_space=pltpu.VMEM),
        scratch_shapes=[
            pltpu.VMEM((chunks, 2, 4, 4, 128, CHUNK), BF16),
            pltpu.VMEM((chunks, 2, 4, 4, 128, CHUNK), BF16),
            pltpu.VMEM((tokens, width), BF16),
            pltpu.VMEM((tokens, width), BF16),
            pltpu.VMEM((rows, feats), BF16),
            pltpu.VMEM((cols, 128), BF16),
            pltpu.VMEM((RANK, width), BF16),
            pltpu.VMEM((RANK, cols), BF16),
            pltpu.VMEM((cols, 2 * RANK), BF16),
            pltpu.VMEM((seqs, RANK, SEQ), F32),
            pltpu.VMEM((2, tokens, CHUNK), F32),
            pltpu.VMEM((tokens, 2 * RANK), F32),
            pltpu.VMEM((4, seqs, 8, 128), F32),
            pltpu.VMEM((4, seqs, 8, 128), F32),
            pltpu.VMEM((2, 4, 4, 64, 128), BF16),
            pltpu.VMEM((STRATA, PAD, feats), BF16),
            pltpu.VMEM((256, 256), BF16),
            pltpu.VMEM((4, rows // (2 * BLOCK), 16, BLOCK), BF16),
            pltpu.VMEM((4, rows // (2 * BLOCK), 16, BLOCK), BF16),
            pltpu.VMEM((4, rows // (2 * BLOCK), 16, BLOCK), BF16),
            pltpu.VMEM((evals, 1), I32),
            dma((6,)),
            dma((chunks,)),
            dma((2, 8)),
            dma((2, 8, chunks)),
            dma((2, 4)),
            dma((2, 2, chunks)),
            dma((3,)),
            dma((3,)),
            dma((16,)),
            dma((16,)),
            dma((2, 3)),
            dma((2, 3)),
            dma((2, 3)),
            dma((2, 3)),
            dma,
            dma,
        ],
        compiler_params=pltpu.CompilerParams(
            collective_id=0, has_side_effects=True, vmem_limit_bytes=57 * 2**20
        ),
    )(
        eval_inputs, eval_grads, w_gate, w_down, proj_in.T, proj_out.T, store_rows,
        eval_strata.reshape(1, evals), block_strata,
    )


def solution(mesh):
    return jax.shard_map(
        local,
        mesh=mesh,
        in_specs=(
            P("store", None),
            P("store", None),
            P("store", "tensor"),
            P("tensor", "store"),
            P(),
            P("tensor", None),
            P("store", "tensor"),
            P(),
            P("store"),
        ),
        out_specs=P("tensor", "store"),
        check_vma=False,
    )
```
